32 devices in a mesh: half: 2 (over core), owner: 16 (over z, y, x).
Axes of the slice: x: 2, y: 2, z: 4, core: 2. Of those that a mesh axis runs over, the one named last changes fastest.
Arguments:
- images: bfloat16 [4096, 16, 512], P(('half', 'owner')), parts along dimension 0, may hold values from -6 to 6
- defocus: bfloat16 [4096], P(('half', 'owner')), parts along dimension 0, may hold values from 1 to 3
- owner_of: int32 [4096, 1], P(('half', 'owner')), parts along dimension 0, may hold values from 0 to 15; in each aligned block of 128 rows (0 to 127, 128 to 255, ...) at most 16 rows name the same one
- pair_of: int32 [4096], P(('half', 'owner')), parts along dimension 0, may hold values from 0 to 31
- shift_of: int32 [4096], P(('half', 'owner')), parts along dimension 0, may hold values from 0 to 127
- projections: bfloat16 [1024, 16, 1024], P(('half', 'owner')), parts along dimension 0, may hold values from -6 to 6
- interp_weights: bfloat16 [1024, 4, 16], P(('half', 'owner')), parts along dimension 0, may hold values from 0 to 0.099609375
- pair_class: int32 [1024], P(('half', 'owner')), parts along dimension 0, may hold values from 0 to 63
Outputs:
- slab: float32 [512, 1024], P(('half', 'owner')), parts along dimension 0
- weights_slab: float32 [512, 512], P(('half', 'owner')), parts along dimension 0
The draws below stay inside these ranges and needn't reach their ends.
There are 2 independent parts, one for each index of `half`. The reference program is written for one: setup_inputs(seed, part) draws one part's arguments, and reference() takes and returns one part's arrays. A program takes and returns all parts, laid end to end along the dimension named above; each array names one. Nothing has to cross between parts.
Inputs may be any that keep to these rules, and one draw needn't show every extreme that they name: `owner_of`: at most 16 particles of one device are assigned to one owner, and that many in some case.
All inputs are finite; a program needn't handle non-finite values.
Results may differ from the reference program's by a relative error of at most 0.0057.
Values may be sent and summed in bfloat16 or wider, within the bound.
No kernel may reach another device: no remote copies, remote signals or barrier semaphores. Data moves between devices by JAX's collectives and lax.ppermute only.
A program may use at most 64 MiB of HBM per device.

```python
import math
import jax
import jax.numpy as jnp
import numpy as np
from jax import lax

BOX = 512
CLASSES = 64
ROWS = 16
SLAB_LINES = 4
SHIFTS = 128
P_DEV = 128
PAIRS_DEV = 32
PARTICLES = 2048
PAIRS = 512
CAP = 16
N_OWNER = 16


def touch_ends(array, rng, smallest, high):
    spot = [jax.random.randint(jax.random.fold_in(rng, axis), (), 0, length) for axis, length in enumerate(array.shape)]
    widest = array.shape.index(max(array.shape))
    neighbour = spot[:widest] + [(spot[widest] + 1) % array.shape[widest]] + spot[widest + 1:]
    return array.at[tuple(spot)].set(smallest).at[tuple(neighbour)].set(high)


def level_of(key, dims, pieces, low, largest):
    def one(position, parts):
        steps = jax.random.uniform(jax.random.fold_in(jax.random.fold_in(key, 6), position), (parts,), jnp.float32, low / len(pieces), largest / len(pieces))
        return jnp.repeat(jnp.exp(steps), dims[position] // parts).reshape((-1,) + (1,) * (len(dims) - position - 1))

    level = one(*pieces[0])
    for cut in pieces[1:]:
        level = level * one(*cut)
    return level


def assign_block(rng, own, number, rows, count, top, limit, lean):
    ranking = jax.random.permutation(rng, count)
    packed, ordinary = load_shares(count, rows * top, limit, lean, True), load_shares(count, rows * top, limit, lean, False)
    places = jnp.arange(count)

    def named(tallies, rotation):
        used = int((tallies > 0).sum())
        fixed = max(1, used // 4)
        shifted = fixed + (places - fixed + rotation * (used - fixed)) % max(1, count - fixed)
        return jnp.zeros((count,), jnp.int32).at[ranking[jnp.where(places < fixed, places, shifted)]].set(jnp.asarray(tallies, jnp.int32))

    tallies = jnp.where(number % 4 == 0, named(packed, number // 4), named(ordinary, number - number // 4 - 1))
    mixed = jax.random.permutation(jax.random.fold_in(own, 3), count)
    donor, receiver = mixed[0:count // 2 * 2:2], mixed[1:count // 2 * 2:2]
    slack = jnp.minimum(tallies[donor] - 1, limit - tallies[receiver]) // 2
    slack = jnp.where((donor == ranking[0]) | (receiver == ranking[0]) | (tallies[receiver] == 0), 0, jnp.maximum(slack, 0))
    shifted = jax.random.randint(jax.random.fold_in(own, 4), (count // 2,), 0, 1 << 20) % (slack + 1)
    tallies = tallies.at[donor].add(-shifted).at[receiver].add(shifted)
    members = jnp.searchsorted(jnp.cumsum(tallies), jnp.arange(rows * top), side="right").astype(jnp.int32)
    listing = members.reshape(top, rows).T
    listing = listing[jax.random.permutation(jax.random.fold_in(own, 1), rows)]
    rotation = jax.random.randint(jax.random.fold_in(own, 2), (rows, 1), 0, top)
    return jnp.take_along_axis(listing, (jnp.arange(top)[None, :] + rotation) % top, axis=1)


def load_shares(number_of, total, limit, lean, full):
    loads = [(1 << 20) // math.isqrt(rank ** lean) + 1 for rank in range(1, number_of + 1)]
    largest = limit if full else min(limit, max(-(-total // number_of), total * loads[0] // sum(loads)))
    least = 1 if total - largest >= number_of - 1 else 0
    holding, surplus = [largest] + [least] * (number_of - 1), total - largest - least * (number_of - 1)
    while surplus > 0:
        movable = [i for i in range(1, number_of) if holding[i] < largest] or [i for i in range(1, number_of) if holding[i] < limit]
        whole, left = sum([loads[i] for i in movable]), surplus
        for i in movable:
            addition = min(limit - holding[i], max(1, left * loads[i] // whole), surplus)
            holding[i] = holding[i] + addition
            surplus = surplus - addition
    return np.array(holding)


def gaussian(own_key, shape, scale, bound, pieces=(), kind=jnp.bfloat16):
    drawn = jax.random.normal(own_key, shape, jnp.float32) * scale
    if len(pieces) > 0:
        drawn = level_of(own_key, shape, pieces, -0.22, 0.18) * drawn
    return jnp.clip(drawn, min=-bound, max=bound).astype(kind)


def setup_inputs(seed: int = 0, part: int = 0) -> dict:
    streams_of = jax.random.split(jax.random.key(seed), 9)
    part_splits = jax.random.split(jax.random.fold_in(streams_of[8], part), 9)
    images = gaussian(part_splits[0], (PARTICLES, ROWS, BOX), 1.0, 6.0, ((0, 16),))
    defocus = jnp.clip(jnp.exp(math.log(3.0) - 1.0986123 * jax.random.uniform(part_splits[1], (PARTICLES,), jnp.float32) ** level_of(part_splits[1], (PARTICLES,), ((0, 16),), -0.2, 0.2)), 1.0, 3.0).astype(jnp.bfloat16)
    owner_of_keys = jax.random.split(jax.random.fold_in(part_splits[2], 1), PARTICLES // P_DEV)
    owner_of_turns = jax.random.permutation(jax.random.fold_in(part_splits[2], 3), PARTICLES // P_DEV)
    owner_of = jax.vmap(lambda own, number: assign_block(jax.random.fold_in(part_splits[2], 2), own, number, P_DEV, N_OWNER, 1, CAP, 1))(owner_of_keys, owner_of_turns).reshape((PARTICLES, 1))
    pair_of = touch_ends(jax.random.randint(part_splits[3], (PARTICLES,), 0, PAIRS_DEV), jax.random.fold_in(part_splits[3], 1), 0, PAIRS_DEV - 1).astype(jnp.int32)
    shift_of = touch_ends(jax.random.randint(part_splits[4], (PARTICLES,), 0, SHIFTS), jax.random.fold_in(part_splits[4], 1), 0, SHIFTS - 1).astype(jnp.int32)
    projections = gaussian(part_splits[5], (PAIRS, ROWS, 2 * BOX), 1.0, 6.0, ((0, 16),))
    interp_weights = jnp.clip(0.099609375 * jax.random.uniform(part_splits[6], (PAIRS, SLAB_LINES, ROWS), jnp.float32) ** level_of(part_splits[6], (PAIRS, SLAB_LINES, ROWS), ((0, 16),), -0.2, 0.2), 0.0, 0.099609375).astype(jnp.bfloat16)
    pair_class = touch_ends(jax.random.randint(part_splits[7], (PAIRS,), 0, CLASSES), jax.random.fold_in(part_splits[7], 1), 0, CLASSES - 1).astype(jnp.int32)
    return {"images": images, "defocus": defocus, "owner_of": owner_of, "pair_of": pair_of, "shift_of": shift_of, "projections": projections, "interp_weights": interp_weights, "pair_class": pair_class}


def dft_table(length):
    column = jnp.arange(length, dtype=jnp.int32)
    product = column[:, None] * column[None, :] % length
    angles = product.astype(jnp.float32) * (2.0 * math.pi / length)
    scaled = jnp.concatenate([jnp.cos(angles), -jnp.sin(angles)], axis=1) / math.sqrt(length)
    return scaled.astype(jnp.bfloat16)

def contrast(defocus_values, length):
    column = jnp.arange(length, dtype=jnp.int32)
    folded = jnp.minimum(column, length - column).astype(jnp.float32) / length
    return -jnp.sin(defocus_values[:, None] * 1500.0 * (folded * folded)[None, :] + 0.2)

def align_weight(spectra, defocus_values, shift_values, references):
    length = spectra.shape[-1] // 2
    line_count = spectra.shape[1]
    factor = contrast(defocus_values, length)[:, None, :]
    column = jnp.arange(length, dtype=jnp.int32)
    angles = (shift_values[:, None] * column[None, :] % length).astype(jnp.float32) * (2.0 * math.pi / length)
    cosine = jnp.cos(angles)[:, None, :]
    sine_part = jnp.sin(angles)[:, None, :]
    real_part = factor * spectra[..., :length].astype(jnp.float32)
    imag_part = factor * spectra[..., length:].astype(jnp.float32)
    aligned_real = real_part * cosine + imag_part * sine_part
    aligned_imag = imag_part * cosine - real_part * sine_part
    scores = lax.optimization_barrier(jnp.sum(aligned_real * references[..., :length].astype(jnp.float32) + aligned_imag * references[..., length:].astype(jnp.float32), axis=(1, 2))) / math.sqrt(line_count * length)
    weight = 1.0 / (1.0 + jnp.exp(-2.0 * scores))
    contrib = (weight[:, None, None] * jnp.concatenate([aligned_real, aligned_imag], axis=-1)).astype(jnp.bfloat16)
    powers = weight[:, None] * factor[:, 0, :] * factor[:, 0, :]
    return (contrib, powers)

def reference(images, defocus, owner_of, pair_of, shift_of, projections, interp_weights, pair_class):
    transform = dft_table(BOX)
    total_pairs = PAIRS_DEV * N_OWNER
    global_pair = (owner_of[:, 0] * PAIRS_DEV + pair_of).astype(jnp.int32)

    def visit_block(running, group_data):
        line_sums, power_sums = running
        block_images, block_defocus, block_pair, block_shift = group_data
        spectra = jnp.dot(block_images.reshape(P_DEV * ROWS, BOX), transform, preferred_element_type=jnp.float32).astype(jnp.bfloat16).reshape(P_DEV, ROWS, 2 * BOX)
        references = jnp.take(projections, block_pair, axis=0)
        contrib, powers = align_weight(spectra, block_defocus.astype(jnp.float32), block_shift, references)
        line_sums = line_sums.at[block_pair].add(contrib.reshape(P_DEV, ROWS * 2 * BOX).astype(jnp.float32))
        power_sums = power_sums.at[block_pair].add(powers)
        return ((line_sums, power_sums), None)
    initial = (jnp.zeros((total_pairs, ROWS * 2 * BOX), jnp.float32), jnp.zeros((total_pairs, BOX), jnp.float32))
    blocks = (images.reshape(N_OWNER, P_DEV, ROWS, BOX), defocus.reshape(N_OWNER, P_DEV), global_pair.reshape(N_OWNER, P_DEV), shift_of.reshape(N_OWNER, P_DEV))
    (line_sums, power_sums), ignored = lax.scan(visit_block, initial, blocks)

    def project(running, group_data):
        block_lines, block_power, block_interp, block_class = group_data
        interp_float = block_interp.astype(jnp.float32)
        image_part = jnp.einsum('pvr,prk->pvk', interp_float, block_lines.reshape(PAIRS_DEV, ROWS, 2 * BOX), precision=lax.Precision.HIGHEST)
        power_part = lax.optimization_barrier(jnp.sum(interp_float, axis=2))[:, :, None] * block_power[:, None, :]
        combined = jnp.concatenate([image_part, power_part], axis=2)
        selector = (block_class[None, :] == jnp.arange(CLASSES, dtype=jnp.int32)[:, None]).astype(jnp.float32)
        return (running + jnp.einsum('cp,pvk->cvk', selector, combined, precision=lax.Precision.HIGHEST), None)
    pair_blocks = (line_sums.reshape(N_OWNER, PAIRS_DEV, ROWS * 2 * BOX), power_sums.reshape(N_OWNER, PAIRS_DEV, BOX), interp_weights.reshape(N_OWNER, PAIRS_DEV, SLAB_LINES, ROWS), pair_class.reshape(N_OWNER, PAIRS_DEV))
    totals, ignored = lax.scan(project, jnp.zeros((CLASSES, SLAB_LINES, 3 * BOX), jnp.float32), pair_blocks)
    totals = totals.reshape(CLASSES * SLAB_LINES, 3 * BOX)
    return (totals[:, :2 * BOX], totals[:, 2 * BOX:] * (CLASSES / (P_DEV * N_OWNER)))
```

```python
import math

import jax
import jax.numpy as jnp
import numpy as np
from jax import lax
from jax.experimental import pallas as pl
from jax.experimental.pallas import tpu as pltpu
from jax.sharding import PartitionSpec as P

CLASSES = 64
F32 = jnp.float32
BF16 = jnp.bfloat16
VMEM_LIMIT = 48 * 1024 * 1024


def packed_table(length):
    half = length // 2
    product = np.arange(length)[:, None] * np.arange(half + 1)[None, :] % length
    angles = product * (2.0 * math.pi / length)
    cosine, sine = np.cos(angles), -np.sin(angles)
    sine[:, 0] = cosine[:, half]
    table = np.concatenate([cosine[:, :half], sine[:, :half]], axis=1) / math.sqrt(length)
    return jnp.asarray(table, F32).astype(BF16)


def mirror(half):
    row = lax.broadcasted_iota(jnp.int32, (half, half), 0)
    column = lax.broadcasted_iota(jnp.int32, (half, half), 1)
    return jnp.where(row + column == half, 1.0, 0.0).astype(BF16)


def fold_kernel(x_ref, out_ref):
    half = x_ref.shape[1] // 4
    flip = mirror(half)
    real_low, real_high = x_ref[:, :half], x_ref[:, half : 2 * half]
    imag_low, imag_high = x_ref[:, 2 * half : 3 * half], x_ref[:, 3 * half :]
    real = real_low.astype(F32) + jnp.dot(real_high, flip, preferred_element_type=F32)
    imag = imag_low.astype(F32) - jnp.dot(imag_high, flip, preferred_element_type=F32)
    lane = lax.broadcasted_iota(jnp.int32, imag.shape, 1)
    imag = jnp.where(lane == 0, real_high.astype(F32)[:, :1], imag)
    out_ref[:, :half] = real.astype(BF16)
    out_ref[:, half:] = imag.astype(BF16)


def fold(projections):
    pairs, lines, width = projections.shape
    return pl.pallas_call(
        fold_kernel,
        grid=(lines,),
        in_specs=[pl.BlockSpec((pairs, width), lambda r: (0, r))],
        out_specs=pl.BlockSpec((pairs, width // 2), lambda r: (0, r)),
        out_shape=jax.ShapeDtypeStruct((pairs, lines * width // 2), BF16),
        name="fold_projections",
    )(projections.reshape(pairs, lines * width))


def factors(defocus, shift, length):
    half = length // 2
    column = jnp.arange(half + 128, dtype=jnp.int32)
    folded = column.astype(F32) / length
    ctf = -jnp.sin(defocus[:, None] * 1500.0 * (folded * folded)[None, :] + 0.2)
    angles = (shift[:, None] * column[None, :half] % length).astype(F32) * (2.0 * math.pi / length)
    nyquist = ctf[:, half] * (1 - 2 * (shift % 2)).astype(F32)
    cosine = ctf[:, :half] * jnp.cos(angles)
    sine = ctf[:, :half] * jnp.sin(angles)
    cosine_imag = jnp.where(column[None, :half] == 0, nyquist[:, None], cosine)
    keep = (column <= half)[None, :]
    return cosine, cosine_imag, sine, jnp.where(keep, ctf * ctf, 0.0).astype(BF16)


def score_kernel(
    scale, x_ref, table_ref, cos_ref, cosi_ref, sin_ref, power_ref, ref_ref, interp_ref,
    class_ref, pair_ref, valid_ref, out_ref, aligned, scores,
):
    step = pl.program_id(0)
    lines = pl.num_programs(0)
    half = cos_ref.shape[1]
    pairs, slots = scores.shape
    spectra = jnp.dot(x_ref[...], table_ref[...], preferred_element_type=F32)
    real, imag = spectra[:, :half], spectra[:, half:]
    sine = sin_ref[...]
    aligned[step, :, :half] = (cos_ref[...] * real + sine * imag).astype(BF16)
    aligned[step, :, half:] = (cosi_ref[...] * imag - sine * real).astype(BF16)
    term = lax.dot_general(
        ref_ref[...], aligned[step], (((1,), (1,)), ((), ())), preferred_element_type=F32
    )

    @pl.when(step == 0)
    def _():
        scores[...] = term

    @pl.when(step > 0)
    def _():
        scores[...] += term

    @pl.when(step == lines - 1)
    def _():
        chosen = lax.broadcasted_iota(jnp.int32, (pairs, slots), 0) == pair_ref[...]
        total = jnp.sum(jnp.where(chosen, scores[...], 0.0), axis=0, keepdims=True)
        weight = valid_ref[...] / (1.0 + jnp.exp(total * (-2.0 * scale)))
        onehot = jnp.where(chosen, 1.0, 0.0).astype(BF16)
        taps = jnp.dot(interp_ref[...], onehot, preferred_element_type=F32)
        label = jnp.dot(class_ref[...], onehot, preferred_element_type=F32)[:1]
        rows = out_ref.shape[0]
        group = lax.broadcasted_iota(jnp.int32, (rows, slots), 0) // (rows // CLASSES)
        spread = jnp.where(group == label.astype(jnp.int32), weight, 0.0).reshape(rows // 8, 8, slots)
        slab = jnp.zeros((rows, 2 * half), F32)
        tap_sum = jnp.zeros((8, slots), F32)
        for line in range(taps.shape[0] // 8):
            tap = taps[line * 8 : line * 8 + 8]
            tap_sum = tap_sum + tap
            mixer = (spread * tap[None]).reshape(rows, slots).astype(BF16)
            slab = slab + jnp.dot(mixer, aligned[line], preferred_element_type=F32)
        mixer = (spread * tap_sum[None]).reshape(rows, slots).astype(BF16)
        out_ref[:, : 2 * half] = slab.astype(BF16)
        out_ref[:, 2 * half :] = jnp.dot(mixer, power_ref[...], preferred_element_type=F32).astype(BF16)


def score_and_spread(images, tables, references, interp, classes, pair, valid, rows):
    cosine, cosine_imag, sine, power = tables
    slots, pairs = images.shape[0], references.shape[0]
    half = cosine.shape[1]
    length = 2 * half
    lines = images.shape[1] // length
    whole = lambda a: pl.BlockSpec(a.shape, lambda r: (0,) * a.ndim)
    line = lambda n: pl.BlockSpec((n, length), lambda r: (0, r))
    table = packed_table(length)
    small = [table, cosine, cosine_imag, sine, power]
    tail = [interp, classes, pair, valid]
    width = length + power.shape[1]
    return pl.pallas_call(
        lambda *refs: score_kernel(1.0 / math.sqrt(lines * length), *refs),
        grid=(lines,),
        in_specs=[line(slots)] + [whole(a) for a in small] + [line(pairs)] + [whole(a) for a in tail],
        out_specs=pl.BlockSpec((rows, width), lambda r: (0, 0)),
        out_shape=jax.ShapeDtypeStruct((rows, width), BF16),
        scratch_shapes=[pltpu.VMEM((lines, slots, length), BF16), pltpu.VMEM((pairs, slots), F32)],
        compiler_params=pltpu.CompilerParams(vmem_limit_bytes=VMEM_LIMIT),
        name="score_and_spread",
    )(images, *small, references, *tail)


def finish_kernel(scale, x_ref, slab_ref, weights_ref):
    half = weights_ref.shape[1] // 2
    total = jnp.sum(x_ref[...].astype(F32), axis=0)
    flip = mirror(half)

    def mirrored(part):
        out = jnp.zeros(part.shape, F32)
        for _ in range(3):
            piece = part.astype(BF16)
            out = out + jnp.dot(piece, flip, preferred_element_type=F32)
            part = part - piece.astype(F32)
        return out

    real, imag, power = total[:, :half], total[:, half : 2 * half], total[:, 2 * half : 3 * half] * scale
    first = lax.broadcasted_iota(jnp.int32, real.shape, 1) == 0
    slab_ref[:, :half] = real
    slab_ref[:, half : 2 * half] = jnp.where(first, imag[:, :1], mirrored(real))
    slab_ref[:, 2 * half : 3 * half] = jnp.where(first, 0.0, imag)
    slab_ref[:, 3 * half :] = jnp.where(first, 0.0, -mirrored(imag))
    weights_ref[:, :half] = power
    weights_ref[:, half:] = jnp.where(first, total[:, 3 * half : 3 * half + 1] * scale, mirrored(power))


def finish(received, length, scale):
    rows = received.shape[1]
    return pl.pallas_call(
        lambda *refs: finish_kernel(scale, *refs),
        out_shape=(
            jax.ShapeDtypeStruct((rows, 2 * length), F32),
            jax.ShapeDtypeStruct((rows, length), F32),
        ),
        name="finish_slab",
    )(received)


def on_device(
    images, defocus, owner_of, pair_of, shift_of, projections, interp_weights, pair_class
):
    particles, lines, length = images.shape
    owners = lax.axis_size("owner")
    capacity = 2 * particles // owners
    slots = owners * capacity
    pairs, slab_lines, _ = interp_weights.shape
    rows = CLASSES * slab_lines
    owner = owner_of[:, 0]
    hits = (owner[:, None] == jnp.arange(owners, dtype=jnp.int32)[None, :]).astype(BF16)
    below = jnp.tril(jnp.ones((particles, particles), BF16), -1)
    earlier = jnp.dot(below, hits, preferred_element_type=F32)
    place = owner * capacity + jnp.sum(earlier * hits.astype(F32), axis=1).astype(jnp.int32)
    pick = (place[None, :] == jnp.arange(slots, dtype=jnp.int32)[:, None]).astype(BF16)
    details = jnp.stack(
        [defocus, pair_of.astype(BF16), shift_of.astype(BF16), jnp.ones_like(defocus)], axis=1
    )
    details = jnp.pad(details, ((0, 0), (0, 124)))
    payload = jnp.concatenate([images.reshape(particles, lines * length), details], axis=1)
    packed = jnp.dot(pick, payload, preferred_element_type=F32).astype(BF16)
    arrived = lax.all_to_all(packed, "owner", split_axis=0, concat_axis=0, tiled=True)
    found = arrived[:, lines * length :].astype(F32)
    pair, shift = found[:, 1].astype(jnp.int32), found[:, 2].astype(jnp.int32)
    tables = factors(found[:, 0], shift, length)
    references = fold(projections)
    repeat = 8 // slab_lines
    interp = jnp.tile(interp_weights.transpose(2, 1, 0), (1, repeat, 1)).reshape(lines * 8, pairs)
    classes = jnp.broadcast_to(pair_class.astype(BF16)[None, :], (8, pairs))
    partial = score_and_spread(
        arrived, tables, references, interp, classes, pair[None, :], found[:, 3][None, :], rows
    )
    received = lax.all_to_all(partial, "owner", split_axis=0, concat_axis=0, tiled=True)
    return finish(
        received.reshape(owners, rows // owners, -1), length, CLASSES / (particles * owners)
    )


def solution(mesh):
    return jax.shard_map(
        on_device,
        mesh=mesh,
        in_specs=(
            P(("half", "owner"), None, None),
            P(("half", "owner")),
            P(("half", "owner"), None),
            P(("half", "owner")),
            P(("half", "owner")),
            P(("half", "owner"), None, None),
            P(("half", "owner"), None, None),
            P(("half", "owner")),
        ),
        out_specs=(P(("half", "owner"), None), P(("half", "owner"), None)),
        check_vma=False,
    )
```

```python
import math

import jax
import jax.numpy as jnp
import numpy as np
from jax import lax
from jax.experimental import pallas as pl
from jax.experimental.pallas import tpu as pltpu
from jax.sharding import PartitionSpec as P

CLASSES = 64
F32 = jnp.float32
BF16 = jnp.bfloat16
VMEM_LIMIT = 48 * 1024 * 1024


def packed_table(length):
    half = length // 2
    product = np.arange(length)[:, None] * np.arange(half + 1)[None, :] % length
    angles = product * (2.0 * math.pi / length)
    cosine, sine = np.cos(angles), -np.sin(angles)
    sine[:, 0] = cosine[:, half]
    table = np.concatenate([cosine[:, :half], sine[:, :half]], axis=1) / math.sqrt(length)
    return jnp.asarray(table, F32).astype(BF16)


def mirror(half):
    row = lax.broadcasted_iota(jnp.int32, (half, half), 0)
    column = lax.broadcasted_iota(jnp.int32, (half, half), 1)
    return jnp.where(row + column == half, 1.0, 0.0).astype(BF16)


def put_tiles(ref, values):
    for t in range(ref.shape[0]):
        ref[t] = values[:, t * 128 : (t + 1) * 128]


def every(ref, start, count, stride):
    picked = [ref[t, pl.ds(start, count, stride=stride), :] for t in range(ref.shape[0])]
    return jnp.concatenate(picked, axis=1)


def fold_kernel(x_ref, info_ref, out_ref, folded):
    pairs, width = out_ref.shape
    half = x_ref.shape[1] // 4
    lines = x_ref.shape[0] // pairs
    flip = mirror(half)
    real_low, real_high = x_ref[:, :half], x_ref[:, half : 2 * half]
    imag_low, imag_high = x_ref[:, 2 * half : 3 * half], x_ref[:, 3 * half :]
    real = real_low.astype(F32) + jnp.dot(real_high, flip, preferred_element_type=F32)
    imag = imag_low.astype(F32) - jnp.dot(imag_high, flip, preferred_element_type=F32)
    lane = lax.broadcasted_iota(jnp.int32, imag.shape, 1)
    imag = jnp.where(lane == 0, real_high.astype(F32)[:, :1], imag)
    put_tiles(folded, jnp.concatenate([real, imag], axis=1))
    for line in range(lines):
        out_ref[:, line * 2 * half : (line + 1) * 2 * half] = every(
            folded, line, pairs, lines
        ).astype(BF16)
    out_ref[:, lines * 2 * half :] = info_ref[...]


def fold(projections, info):
    pairs, lines, width = projections.shape
    return pl.pallas_call(
        fold_kernel,
        out_shape=jax.ShapeDtypeStruct((pairs, lines * width // 2 + info.shape[1]), BF16),
        scratch_shapes=[pltpu.VMEM((width // 256, pairs * lines, 128), F32)],
        compiler_params=pltpu.CompilerParams(vmem_limit_bytes=VMEM_LIMIT),
        name="fold_projections",
    )(projections.reshape(pairs * lines, width), info)


def sort_kernel(capacity, x_ref, bin_ref, pair_ref, shift_ref, defocus_ref, *refs):
    outs, facts_ref, wide = refs[:-2], refs[-2], refs[-1]
    particles = bin_ref.shape[1]
    length = x_ref.shape[1]
    lines = x_ref.shape[0] // particles
    slots = facts_ref.shape[1]
    bins = -(-(slots // capacity) // 8) * 8
    hits = lax.broadcasted_iota(jnp.int32, (bins, particles), 0) == bin_ref[...]
    row = lax.broadcasted_iota(jnp.int32, (particles, particles), 0)
    column = lax.broadcasted_iota(jnp.int32, (particles, particles), 1)
    before = jnp.where(row < column, 1.0, 0.0).astype(BF16)
    earlier = jnp.dot(jnp.where(hits, 1.0, 0.0).astype(BF16), before, preferred_element_type=F32)
    earlier = jnp.sum(jnp.where(hits, earlier, 0.0), axis=0, keepdims=True)
    place = bin_ref[...] * capacity + earlier.astype(jnp.int32)
    pick = lax.broadcasted_iota(jnp.int32, (slots, particles), 0) == place
    pick = jnp.where(pick, 1.0, 0.0).astype(BF16)
    kind = lax.broadcasted_iota(jnp.int32, (8, particles), 0)
    facts = jnp.where(kind == 0, defocus_ref[...], jnp.ones((8, particles), F32))
    facts = jnp.where(kind == 1, pair_ref[...].astype(F32), facts)
    facts = jnp.where(kind == 2, shift_ref[...].astype(F32), facts).astype(BF16)
    facts_ref[...] = lax.dot_general(
        facts, pick, (((1,), (1,)), ((), ())), preferred_element_type=F32
    )
    put_tiles(wide, x_ref[...].astype(F32))
    for line in range(lines):
        picked = jnp.dot(
            pick, every(wide, line, particles, lines).astype(BF16), preferred_element_type=F32
        ).astype(BF16)
        each = slots // len(outs)
        for i, out_ref in enumerate(outs):
            out_ref[:, line * length : (line + 1) * length] = picked[i * each : (i + 1) * each]


def sort_particles(images, bins, pair, shift, defocus, count, capacity, pieces):
    particles, lines, length = images.shape
    slots = count * capacity
    return pl.pallas_call(
        lambda *refs: sort_kernel(capacity, *refs),
        out_shape=[jax.ShapeDtypeStruct((slots // pieces, lines * length), BF16)] * pieces
        + [jax.ShapeDtypeStruct((8, slots), F32)],
        scratch_shapes=[pltpu.VMEM((length // 128, particles * lines, 128), F32)],
        compiler_params=pltpu.CompilerParams(vmem_limit_bytes=VMEM_LIMIT),
        name="sort_particles",
    )(
        images.reshape(particles * lines, length),
        bins[None, :], pair[None, :], shift[None, :], defocus.astype(F32)[None, :],
    )


def factors(defocus, shift, length):
    half = length // 2
    column = jnp.arange(half + 128, dtype=jnp.int32)
    folded = column.astype(F32) / length
    ctf = -jnp.sin(defocus[:, None] * 1500.0 * (folded * folded)[None, :] + 0.2)
    angles = (shift[:, None] * column[None, :half] % length).astype(F32) * (2.0 * math.pi / length)
    nyquist = ctf[:, half] * (1 - 2 * (shift % 2)).astype(F32)
    cosine = ctf[:, :half] * jnp.cos(angles)
    sine = ctf[:, :half] * jnp.sin(angles)
    cosine_imag = jnp.where(column[None, :half] == 0, nyquist[:, None], cosine)
    keep = (column <= half)[None, :]
    return cosine, cosine_imag, sine, jnp.where(keep, ctf * ctf, 0.0).astype(BF16)


def score_kernel(scale, n_images, n_refs, slab_lines, *refs):
    images, refs = refs[:n_images], refs[n_images:]
    blocks, refs = refs[:n_refs], refs[n_refs:]
    infos, refs = refs[:n_refs], refs[n_refs:]
    table_ref, cos_ref, cosi_ref, sin_ref, power_ref, facts_ref, out_ref, aligned, scores, taps, spread = refs
    step = pl.program_id(0)
    half = cos_ref.shape[1]
    pairs, slots = scores.shape
    rows = out_ref.shape[0]
    length = 2 * half
    lines = aligned.shape[0]
    here = images[0].shape[1] // length

    def chosen():
        pair = facts_ref[1:2, :].astype(jnp.int32)
        return lax.broadcasted_iota(jnp.int32, (pairs, slots), 0) == pair

    @pl.when(step == 0)
    def _():
        scores[...] = jnp.zeros(scores.shape, F32)
        onehot = jnp.where(chosen(), 1.0, 0.0).astype(BF16)
        info = jnp.concatenate([ref[...] for ref in infos], axis=0)
        found = lax.dot_general(
            info, onehot, (((0,), (0,)), ((), ())), preferred_element_type=F32
        )
        put_tiles(taps, found)
        label = found[slab_lines * lines : slab_lines * lines + 1, :].astype(jnp.int32)
        group = lax.broadcasted_iota(jnp.int32, (rows, slots), 0) // (rows // CLASSES)
        spread[...] = jnp.where(group == label, 1.0, 0.0)

    sine = sin_ref[...]
    total = scores[...]
    for i in range(here):
        at = slice(i * length, (i + 1) * length)
        lines_in = jnp.concatenate([ref[:, at] for ref in images], axis=0)
        spectra = jnp.dot(lines_in, table_ref[...], preferred_element_type=F32)
        spectra = spectra.astype(BF16).astype(F32)
        real, imag = spectra[:, :half], spectra[:, half:]
        turned = jnp.concatenate(
            [cos_ref[...] * real + sine * imag, cosi_ref[...] * imag - sine * real], axis=1
        )
        aligned[step * here + i] = turned
        against = jnp.concatenate([ref[:, at] for ref in blocks], axis=0)
        total = total + lax.dot_general(
            against, turned.astype(BF16), (((1,), (1,)), ((), ())), preferred_element_type=F32
        )
    scores[...] = total

    @pl.when(step == pl.num_programs(0) - 1)
    def _():
        score = jnp.sum(jnp.where(chosen(), scores[...], 0.0), axis=0, keepdims=True)
        weight = facts_ref[3:4, :] / (1.0 + jnp.exp(score * (-2.0 * scale)))
        upright = jnp.broadcast_to(weight, (128, slots)).T
        upright = jnp.concatenate([upright] * (length // 128), axis=1)
        slab = jnp.zeros((rows, length), F32)
        tap_sum = jnp.zeros((slab_lines, slots), F32)
        mask = spread[...].reshape(rows // 8, 8, slots)
        for line in range(lines):
            tap = every(taps, line, slab_lines, lines)
            tap_sum = tap_sum + tap
            tap = jnp.concatenate([tap] * (8 // slab_lines), axis=0)
            mixer = (mask * tap[None]).reshape(rows, slots).astype(BF16)
            contrib = (upright * aligned[line]).astype(BF16)
            slab = slab + jnp.dot(mixer, contrib, preferred_element_type=F32)
        tap = jnp.concatenate([tap_sum * weight] * (8 // slab_lines), axis=0)
        mixer = (mask * tap[None]).reshape(rows, slots).astype(BF16)
        out_ref[:, :length] = slab.astype(BF16)
        out_ref[:, length:] = jnp.dot(mixer, power_ref[...], preferred_element_type=F32).astype(BF16)


def score_and_spread(images, references, facts, tables, rows, slab_lines, lines, length):
    slots = sum(a.shape[0] for a in images)
    pairs = sum(a.shape[0] for a in references)
    here = 4
    whole = lambda a: pl.BlockSpec(a.shape, lambda r: (0,) * a.ndim)
    line = lambda a: pl.BlockSpec((a.shape[0], here * length), lambda r: (0, r))
    info = lambda a: pl.BlockSpec((a.shape[0], 128), lambda r: (0, lines * length // 128))
    small = [packed_table(length), *tables, facts]
    width = length + tables[3].shape[1]
    return pl.pallas_call(
        lambda *refs: score_kernel(
            1.0 / math.sqrt(lines * length), len(images), len(references), slab_lines, *refs
        ),
        grid=(lines // here,),
        in_specs=[line(a) for a in images] + [line(a) for a in references]
        + [info(a) for a in references] + [whole(a) for a in small],
        out_specs=pl.BlockSpec((rows, width), lambda r: (0, 0)),
        out_shape=jax.ShapeDtypeStruct((rows, width), BF16),
        scratch_shapes=[
            pltpu.VMEM((lines, slots, length), F32),
            pltpu.VMEM((pairs, slots), F32),
            pltpu.VMEM((slots // 128, 128, 128), F32),
            pltpu.VMEM((rows, slots), F32),
        ],
        compiler_params=pltpu.CompilerParams(vmem_limit_bytes=VMEM_LIMIT),
        name="score_and_spread",
    )(*images, *references, *references, *small)


def finish_kernel(scale, x_ref, slab_ref, weights_ref):
    half = weights_ref.shape[1] // 2
    total = jnp.sum(x_ref[...].astype(F32), axis=0)
    flip = mirror(half)

    def mirrored(part):
        out = jnp.zeros(part.shape, F32)
        for _ in range(3):
            piece = part.astype(BF16)
            out = out + jnp.dot(piece, flip, preferred_element_type=F32)
            part = part - piece.astype(F32)
        return out

    real, imag, power = total[:, :half], total[:, half : 2 * half], total[:, 2 * half : 3 * half] * scale
    first = lax.broadcasted_iota(jnp.int32, real.shape, 1) == 0
    slab_ref[:, :half] = real
    slab_ref[:, half : 2 * half] = jnp.where(first, imag[:, :1], mirrored(real))
    slab_ref[:, 2 * half : 3 * half] = jnp.where(first, 0.0, imag)
    slab_ref[:, 3 * half :] = jnp.where(first, 0.0, -mirrored(imag))
    weights_ref[:, :half] = power
    weights_ref[:, half:] = jnp.where(first, total[:, 3 * half : 3 * half + 1] * scale, mirrored(power))


def finish(received, length, scale):
    rows = received.shape[1]
    return pl.pallas_call(
        lambda *refs: finish_kernel(scale, *refs),
        out_shape=(
            jax.ShapeDtypeStruct((rows, 2 * length), F32),
            jax.ShapeDtypeStruct((rows, length), F32),
        ),
        name="finish_slab",
    )(received)


def on_device(
    images, defocus, owner_of, pair_of, shift_of, projections, interp_weights, pair_class
):
    particles, lines, length = images.shape
    owners = lax.axis_size("owner")
    capacity = 2 * particles // owners
    pairs, slab_lines, _ = interp_weights.shape
    rows = CLASSES * slab_lines
    reach = max(1, capacity // 4)
    count = owners // reach
    here = lax.axis_index("owner")
    owner = owner_of[:, 0]
    pair = (here // count - owner // count) % reach * pairs + pair_of
    info = jnp.concatenate(
        [
            interp_weights.reshape(pairs, slab_lines * lines),
            pair_class.astype(BF16)[:, None],
            jnp.zeros((pairs, 127 - slab_lines * lines), BF16),
        ],
        axis=1,
    )
    references = [fold(projections, info)]
    for shift in range(1, reach):
        ring = [(i, (i + shift * count) % owners) for i in range(owners)]
        references.append(lax.ppermute(references[0], "owner", ring))
    columns = owner % count
    if reach > 1:
        *sorted_lines, facts = sort_particles(
            images, columns ^ here % count, pair, shift_of, defocus, count, reach * capacity, count
        )
        swap = lambda a, i: lax.ppermute(a, "owner", [(k, k ^ i) for k in range(owners)]) if i else a
        arrived = [swap(a, i) for i, a in enumerate(sorted_lines)]
        facts = jnp.concatenate(
            [swap(a, i) for i, a in enumerate(jnp.split(facts, count, axis=1))], axis=1
        )
    else:
        sorted_lines, facts = sort_particles(
            images, columns, pair, shift_of, defocus, count, capacity, 1
        )
        send = lambda a: lax.all_to_all(a, "owner", split_axis=0, concat_axis=0, tiled=True)
        arrived, facts = [send(sorted_lines)], send(facts.T).T
    tables = factors(facts[0], facts[2].astype(jnp.int32), length)
    partial = score_and_spread(
        arrived, references, facts, tables, rows, slab_lines, lines, length
    )
    received = lax.all_to_all(partial, "owner", split_axis=0, concat_axis=0, tiled=True)
    return finish(
        received.reshape(owners, rows // owners, -1), length, CLASSES / (particles * owners)
    )


def solution(mesh):
    return jax.shard_map(
        on_device,
        mesh=mesh,
        in_specs=(
            P(("half", "owner"), None, None),
            P(("half", "owner")),
            P(("half", "owner"), None),
            P(("half", "owner")),
            P(("half", "owner")),
            P(("half", "owner"), None, None),
            P(("half", "owner"), None, None),
            P(("half", "owner")),
        ),
        out_specs=(P(("half", "owner"), None), P(("half", "owner"), None)),
        check_vma=False,
    )
```

```python
import math

import jax
import jax.numpy as jnp
import numpy as np
from jax import lax
from jax.experimental import pallas as pl
from jax.experimental.pallas import tpu as pltpu
from jax.sharding import PartitionSpec as P

CLASSES = 64
F32 = jnp.float32
BF16 = jnp.bfloat16
VMEM_LIMIT = 48 * 1024 * 1024


def packed_table(length):
    half = length // 2
    product = np.arange(length)[:, None] * np.arange(half + 1)[None, :] % length
    angles = product * (2.0 * math.pi / length)
    cosine, sine = np.cos(angles), -np.sin(angles)
    sine[:, 0] = cosine[:, half]
    table = np.concatenate([cosine[:, :half], sine[:, :half]], axis=1) / math.sqrt(length)
    return jnp.asarray(table, F32).astype(BF16)


def mirror(half):
    row = lax.broadcasted_iota(jnp.int32, (half, half), 0)
    column = lax.broadcasted_iota(jnp.int32, (half, half), 1)
    return jnp.where(row + column == half, 1.0, 0.0).astype(BF16)


def put_tiles(ref, values):
    for t in range(ref.shape[0]):
        ref[t] = values[:, t * 128 : (t + 1) * 128]


def every(ref, start, count, stride):
    picked = [ref[t, pl.ds(start, count, stride=stride), :] for t in range(ref.shape[0])]
    return jnp.concatenate(picked, axis=1)


def fold_kernel(x_ref, info_ref, out_ref, folded):
    pairs, width = out_ref.shape
    half = x_ref.shape[1] // 4
    lines = x_ref.shape[0] // pairs
    flip = mirror(half)
    real_low, real_high = x_ref[:, :half], x_ref[:, half : 2 * half]
    imag_low, imag_high = x_ref[:, 2 * half : 3 * half], x_ref[:, 3 * half :]
    real = real_low.astype(F32) + jnp.dot(real_high, flip, preferred_element_type=F32)
    imag = imag_low.astype(F32) - jnp.dot(imag_high, flip, preferred_element_type=F32)
    lane = lax.broadcasted_iota(jnp.int32, imag.shape, 1)
    imag = jnp.where(lane == 0, real_high.astype(F32)[:, :1], imag)
    put_tiles(folded, jnp.concatenate([real, imag], axis=1))
    for line in range(lines):
        out_ref[:, line * 2 * half : (line + 1) * 2 * half] = every(
            folded, line, pairs, lines
        ).astype(BF16)
    out_ref[:, lines * 2 * half :] = info_ref[...]


def fold(projections, info):
    pairs, lines, width = projections.shape
    return pl.pallas_call(
        fold_kernel,
        out_shape=jax.ShapeDtypeStruct((pairs, lines * width // 2 + info.shape[1]), BF16),
        scratch_shapes=[pltpu.VMEM((width // 256, pairs * lines, 128), F32)],
        compiler_params=pltpu.CompilerParams(vmem_limit_bytes=VMEM_LIMIT),
        name="fold_projections",
    )(projections.reshape(pairs * lines, width), info)


def sort_kernel(reach, count, capacity, pairs, x_ref, owner_ref, pair_ref, shift_ref, defocus_ref, *refs):
    *outs, wide, pick_ref = refs
    pieces = len(outs) // 2
    outs, facts_refs = outs[:pieces], outs[pieces:]
    particles = owner_ref.shape[1]
    length = x_ref.shape[1]
    lines = x_ref.shape[0] // particles
    slots = pick_ref.shape[0]
    each = slots // pieces

    @pl.when(pl.program_id(0) == 0)
    def _():
        me = lax.axis_index("owner")
        owner = owner_ref[...]
        bins = owner & (count - 1)
        if pieces > 1:
            bins = bins ^ (me & (count - 1))
        step = ((me >> (count.bit_length() - 1)) - (owner >> (count.bit_length() - 1))) & (reach - 1)
        pair = step * pairs + pair_ref[...]
        padded = -(-count // 8) * 8
        hits = lax.broadcasted_iota(jnp.int32, (padded, particles), 0) == bins
        row = lax.broadcasted_iota(jnp.int32, (particles, particles), 0)
        column = lax.broadcasted_iota(jnp.int32, (particles, particles), 1)
        before = jnp.where(row < column, 1.0, 0.0).astype(BF16)
        earlier = jnp.dot(
            jnp.where(hits, 1.0, 0.0).astype(BF16), before, preferred_element_type=F32
        )
        earlier = jnp.sum(jnp.where(hits, earlier, 0.0), axis=0, keepdims=True)
        place = bins * capacity + earlier.astype(jnp.int32)
        pick = lax.broadcasted_iota(jnp.int32, (slots, particles), 0) == place
        pick_ref[...] = jnp.where(pick, 1.0, 0.0).astype(BF16)
        kind = lax.broadcasted_iota(jnp.int32, (8, particles), 0)
        facts = jnp.where(kind == 0, defocus_ref[...].astype(F32), jnp.ones((8, particles), F32))
        facts = jnp.where(kind == 1, pair.astype(F32), facts)
        facts = jnp.where(kind == 2, shift_ref[...].astype(F32), facts).astype(BF16)
        for i, facts_ref in enumerate(facts_refs):
            facts_ref[...] = lax.dot_general(
                facts,
                pick_ref[i * each : (i + 1) * each],
                (((1,), (1,)), ((), ())),
                preferred_element_type=F32,
            )
        put_tiles(wide, x_ref[...].astype(F32))

    here = outs[0].shape[1] // length
    for i in range(here):
        line = pl.program_id(0) * here + i
        rows = every(wide, line, particles, lines).astype(BF16)
        picked = jnp.dot(pick_ref[...], rows, preferred_element_type=F32).astype(BF16)
        for j, out_ref in enumerate(outs):
            out_ref[:, i * length : (i + 1) * length] = picked[j * each : (j + 1) * each]


def sort_particles(images, owner, pair, shift, defocus, reach, count, capacity, pairs, pieces):
    particles, lines, length = images.shape
    slots = count * capacity
    each = slots // pieces
    here = 4
    whole = lambda a: pl.BlockSpec(a.shape, lambda r: (0,) * a.ndim)
    args = [images.reshape(particles * lines, length)] + [a[None, :] for a in (owner, pair, shift, defocus)]
    return pl.pallas_call(
        lambda *refs: sort_kernel(reach, count, capacity, pairs, *refs),
        grid=(lines // here,),
        in_specs=[whole(a) for a in args],
        out_specs=[pl.BlockSpec((each, here * length), lambda r: (0, r))] * pieces
        + [pl.BlockSpec((8, each), lambda r: (0, 0))] * pieces,
        out_shape=[jax.ShapeDtypeStruct((each, lines * length), BF16)] * pieces
        + [jax.ShapeDtypeStruct((8, each), F32)] * pieces,
        scratch_shapes=[
            pltpu.VMEM((length // 128, particles * lines, 128), F32),
            pltpu.VMEM((slots, particles), BF16),
        ],
        compiler_params=pltpu.CompilerParams(vmem_limit_bytes=VMEM_LIMIT),
        name="sort_particles",
    )(*args)


def factors(defocus, shift, length):
    half = length // 2
    column = jnp.arange(half + 128, dtype=jnp.int32)
    folded = column.astype(F32) / length
    ctf = -jnp.sin(defocus[:, None] * 1500.0 * (folded * folded)[None, :] + 0.2)
    angles = (shift[:, None] * column[None, :half] % length).astype(F32) * (2.0 * math.pi / length)
    nyquist = ctf[:, half] * (1 - 2 * (shift % 2)).astype(F32)
    cosine = ctf[:, :half] * jnp.cos(angles)
    sine = ctf[:, :half] * jnp.sin(angles)
    cosine_imag = jnp.where(column[None, :half] == 0, nyquist[:, None], cosine)
    keep = (column <= half)[None, :]
    return cosine, cosine_imag, sine, jnp.where(keep, ctf * ctf, 0.0).astype(BF16)


def joined(refs, sizes, at):
    blocks, start = [], 0
    for size in sizes:
        block = refs[start][:, at]
        for ref in refs[start + 1 : start + size]:
            block = block + ref[:, at]
        blocks.append(block)
        start += size
    return jnp.concatenate(blocks, axis=0)


def score_kernel(scale, n_images, sizes, slab_lines, *refs):
    n_refs = sum(sizes)
    images, refs = refs[:n_images], refs[n_images:]
    blocks, refs = refs[:n_refs], refs[n_refs:]
    infos, refs = refs[:n_refs], refs[n_refs:]
    table_ref, cos_ref, cosi_ref, sin_ref, power_ref, facts_ref, out_ref, aligned, scores, taps, spread = refs
    step = pl.program_id(0)
    half = cos_ref.shape[1]
    pairs, slots = scores.shape
    rows = out_ref.shape[0]
    length = 2 * half
    lines = aligned.shape[0]
    here = images[0].shape[1] // length

    def chosen():
        pair = facts_ref[1:2, :].astype(jnp.int32)
        return lax.broadcasted_iota(jnp.int32, (pairs, slots), 0) == pair

    @pl.when(step == 0)
    def _():
        scores[...] = jnp.zeros(scores.shape, F32)
        onehot = jnp.where(chosen(), 1.0, 0.0).astype(BF16)
        info = joined(infos, sizes, slice(None))
        found = lax.dot_general(
            info, onehot, (((0,), (0,)), ((), ())), preferred_element_type=F32
        )
        put_tiles(taps, found)
        label = found[slab_lines * lines : slab_lines * lines + 1, :].astype(jnp.int32)
        group = lax.broadcasted_iota(jnp.int32, (rows, slots), 0) // (rows // CLASSES)
        spread[...] = jnp.where(group == label, 1.0, 0.0)

    sine = sin_ref[...]
    total = scores[...]
    for i in range(here):
        at = slice(i * length, (i + 1) * length)
        lines_in = jnp.concatenate([ref[:, at] for ref in images], axis=0)
        spectra = jnp.dot(lines_in, table_ref[...], preferred_element_type=F32)
        spectra = spectra.astype(BF16).astype(F32)
        real, imag = spectra[:, :half], spectra[:, half:]
        turned = jnp.concatenate(
            [cos_ref[...] * real + sine * imag, cosi_ref[...] * imag - sine * real], axis=1
        )
        aligned[step * here + i] = turned
        against = joined(blocks, sizes, at)
        total = total + lax.dot_general(
            against, turned.astype(BF16), (((1,), (1,)), ((), ())), preferred_element_type=F32
        )
    scores[...] = total

    @pl.when(step == pl.num_programs(0) - 1)
    def _():
        score = jnp.sum(jnp.where(chosen(), scores[...], 0.0), axis=0, keepdims=True)
        weight = facts_ref[3:4, :] / (1.0 + jnp.exp(score * (-2.0 * scale)))
        upright = jnp.broadcast_to(weight, (128, slots)).T
        upright = jnp.concatenate([upright] * (length // 128), axis=1)
        slab = jnp.zeros((rows, length), F32)
        tap_sum = jnp.zeros((slab_lines, slots), F32)
        mask = spread[...].reshape(rows // 8, 8, slots)
        for line in range(lines):
            tap = every(taps, line, slab_lines, lines)
            tap_sum = tap_sum + tap
            tap = jnp.concatenate([tap] * (8 // slab_lines), axis=0)
            mixer = (mask * tap[None]).reshape(rows, slots).astype(BF16)
            contrib = (upright * aligned[line]).astype(BF16)
            slab = slab + jnp.dot(mixer, contrib, preferred_element_type=F32)
        tap = jnp.concatenate([tap_sum * weight] * (8 // slab_lines), axis=0)
        mixer = (mask * tap[None]).reshape(rows, slots).astype(BF16)
        out_ref[:, :length] = slab.astype(BF16)
        out_ref[:, length:] = jnp.dot(mixer, power_ref[...], preferred_element_type=F32).astype(BF16)


def score_and_spread(images, references, facts, tables, rows, slab_lines, lines, length):
    slots = sum(a.shape[0] for a in images)
    pairs = sum(a[0].shape[0] for a in references)
    sizes = [len(a) for a in references]
    references = [a for blocks in references for a in blocks]
    here = 4
    whole = lambda a: pl.BlockSpec(a.shape, lambda r: (0,) * a.ndim)
    line = lambda a: pl.BlockSpec((a.shape[0], here * length), lambda r: (0, r))
    info = lambda a: pl.BlockSpec((a.shape[0], 128), lambda r: (0, lines * length // 128))
    small = [packed_table(length), *tables, facts]
    width = length + tables[3].shape[1]
    return pl.pallas_call(
        lambda *refs: score_kernel(
            1.0 / math.sqrt(lines * length), len(images), sizes, slab_lines, *refs
        ),
        grid=(lines // here,),
        in_specs=[line(a) for a in images] + [line(a) for a in references]
        + [info(a) for a in references] + [whole(a) for a in small],
        out_specs=pl.BlockSpec((rows, width), lambda r: (0, 0)),
        out_shape=jax.ShapeDtypeStruct((rows, width), BF16),
        scratch_shapes=[
            pltpu.VMEM((lines, slots, length), F32),
            pltpu.VMEM((pairs, slots), F32),
            pltpu.VMEM((slots // 128, 128, 128), F32),
            pltpu.VMEM((rows, slots), F32),
        ],
        compiler_params=pltpu.CompilerParams(vmem_limit_bytes=VMEM_LIMIT),
        name="score_and_spread",
    )(*images, *references, *references, *small)


def finish_kernel(scale, x_ref, slab_ref, weights_ref):
    half = weights_ref.shape[1] // 2
    total = jnp.sum(x_ref[...].astype(F32), axis=0)
    flip = mirror(half)

    def mirrored(part):
        out = jnp.zeros(part.shape, F32)
        for _ in range(3):
            piece = part.astype(BF16)
            out = out + jnp.dot(piece, flip, preferred_element_type=F32)
            part = part - piece.astype(F32)
        return out

    real, imag, power = total[:, :half], total[:, half : 2 * half], total[:, 2 * half : 3 * half] * scale
    first = lax.broadcasted_iota(jnp.int32, real.shape, 1) == 0
    slab_ref[:, :half] = real
    slab_ref[:, half : 2 * half] = jnp.where(first, imag[:, :1], mirrored(real))
    slab_ref[:, 2 * half : 3 * half] = jnp.where(first, 0.0, imag)
    slab_ref[:, 3 * half :] = jnp.where(first, 0.0, -mirrored(imag))
    weights_ref[:, :half] = power
    weights_ref[:, half:] = jnp.where(first, total[:, 3 * half : 3 * half + 1] * scale, mirrored(power))


def finish(received, length, scale):
    rows = received.shape[1]
    return pl.pallas_call(
        lambda *refs: finish_kernel(scale, *refs),
        out_shape=(
            jax.ShapeDtypeStruct((rows, 2 * length), F32),
            jax.ShapeDtypeStruct((rows, length), F32),
        ),
        name="finish_slab",
    )(received)


def gather_rows(block, owners, reach, count):
    turn = lambda i: lax.ppermute(block, "owner", [(k, (k + i * count) % owners) for k in range(owners)])
    if reach != 4:
        return [(block,)] + [(turn(i),) for i in range(1, reach)]
    back, ahead = turn(1), turn(3)
    inner = range(count, 3 * count)
    up = lax.ppermute(back, "owner", [(k, k + count) for k in inner])
    down = lax.ppermute(ahead, "owner", [(k, k - count) for k in inner])
    return [(block,), (back,), (up, down), (ahead,)]


def on_device(
    images, defocus, owner_of, pair_of, shift_of, projections, interp_weights, pair_class
):
    particles, lines, length = images.shape
    owners = lax.axis_size("owner")
    capacity = 2 * particles // owners
    pairs, slab_lines, _ = interp_weights.shape
    rows = CLASSES * slab_lines
    reach = max(1, capacity // 4)
    count = owners // reach
    owner = owner_of[:, 0]
    pieces = count if reach > 1 else 1
    moved = sort_particles(
        images, owner, pair_of, shift_of, defocus, reach, count, reach * capacity, pairs, pieces
    )
    lines_out, facts_out = moved[:pieces], moved[pieces:]
    if reach > 1:
        swap = lambda a, i: lax.ppermute(a, "owner", [(k, k ^ i) for k in range(owners)]) if i else a
        arrived = [swap(a, i) for i, a in enumerate(lines_out)]
        facts = jnp.concatenate([swap(a, i) for i, a in enumerate(facts_out)], axis=1)
    else:
        send = lambda a: lax.all_to_all(a, "owner", split_axis=0, concat_axis=0, tiled=True)
        arrived, facts = [send(lines_out[0])], send(facts_out[0].T).T
    info = jnp.concatenate(
        [
            interp_weights.reshape(pairs, slab_lines * lines),
            pair_class.astype(BF16)[:, None],
            jnp.zeros((pairs, 127 - slab_lines * lines), BF16),
        ],
        axis=1,
    )
    references = gather_rows(fold(projections, info), owners, reach, count)
    tables = factors(facts[0], facts[2].astype(jnp.int32), length)
    partial = score_and_spread(
        arrived, references, facts, tables, rows, slab_lines, lines, length
    )
    received = lax.all_to_all(partial, "owner", split_axis=0, concat_axis=0, tiled=True)
    return finish(
        received.reshape(owners, rows // owners, -1), length, CLASSES / (particles * owners)
    )


def solution(mesh):
    return jax.shard_map(
        on_device,
        mesh=mesh,
        in_specs=(
            P(("half", "owner"), None, None),
            P(("half", "owner")),
            P(("half", "owner"), None),
            P(("half", "owner")),
            P(("half", "owner")),
            P(("half", "owner"), None, None),
            P(("half", "owner"), None, None),
            P(("half", "owner")),
        ),
        out_specs=(P(("half", "owner"), None), P(("half", "owner"), None)),
        check_vma=False,
    )
```

```python
import math

import jax
import jax.numpy as jnp
import numpy as np
from jax import lax
from jax.experimental import pallas as pl
from jax.experimental.pallas import tpu as pltpu
from jax.sharding import PartitionSpec as P

CLASSES = 64
F32 = jnp.float32
BF16 = jnp.bfloat16
HBM = pl.BlockSpec(memory_space=pltpu.MemorySpace.HBM)


def vmem(megabytes):
    return pltpu.CompilerParams(vmem_limit_bytes=megabytes * 1024 * 1024)


def packed_table(length):
    half = length // 2
    product = np.arange(length)[:, None] * np.arange(half + 1)[None, :] % length
    angles = product * (2.0 * math.pi / length)
    cosine, sine = np.cos(angles), -np.sin(angles)
    sine[:, 0] = cosine[:, half]
    table = np.concatenate([cosine[:, :half], sine[:, :half]], axis=1) / math.sqrt(length)
    return jnp.asarray(table, F32).astype(BF16)


def mirror(half):
    row = lax.broadcasted_iota(jnp.int32, (half, half), 0)
    column = lax.broadcasted_iota(jnp.int32, (half, half), 1)
    return jnp.where(row + column == half, 1.0, 0.0).astype(BF16)


def put_tiles(ref, values):
    for t in range(ref.shape[0]):
        ref[t] = values[:, t * 128 : (t + 1) * 128]


def every(ref, start, count, stride):
    picked = [ref[t, pl.ds(start, count, stride=stride), :] for t in range(ref.shape[0])]
    return jnp.concatenate(picked, axis=1)


def flipped(rows):
    down, across = rows.shape
    if across < 128:
        rows = jnp.concatenate([rows, jnp.zeros((down, 128 - across), F32)], axis=1)
    if down < 128:
        rows = jnp.concatenate([rows, jnp.zeros((128 - down, 128), F32)], axis=0)
    return rows.T


def short_sine(x):
    square = x * x
    total = jnp.full(x.shape, -1.0 / 39916800.0, F32)
    for factor in (1.0 / 362880.0, -1.0 / 5040.0, 1.0 / 120.0, -1.0 / 6.0, 1.0):
        total = total * square + factor
    return total * x


def sine_of(x):
    turns = jnp.floor(x * (0.5 / math.pi) + 0.5)
    x = ((x - turns * 6.28125) - turns * 0.0019340515136718750) - turns * 1.2556659145e-06
    x = jnp.where(x > 0.5 * math.pi, math.pi - x, jnp.where(x < -0.5 * math.pi, -math.pi - x, x))
    return short_sine(x)


def fold_kernel(x_ref, interp_ref, class_ref, out_ref, folded):
    pairs, width = out_ref.shape
    half = x_ref.shape[1] // 4
    lines = x_ref.shape[0] // pairs
    flip = mirror(half)
    real_low, real_high = x_ref[:, :half], x_ref[:, half : 2 * half]
    imag_low, imag_high = x_ref[:, 2 * half : 3 * half], x_ref[:, 3 * half :]
    real = real_low.astype(F32) + jnp.dot(real_high, flip, preferred_element_type=F32)
    imag = imag_low.astype(F32) - jnp.dot(imag_high, flip, preferred_element_type=F32)
    lane = lax.broadcasted_iota(jnp.int32, imag.shape, 1)
    imag = jnp.where(lane == 0, real_high.astype(F32)[:, :1], imag)
    put_tiles(folded, jnp.concatenate([real, imag], axis=1))
    for line in range(lines):
        out_ref[:, line * 2 * half : (line + 1) * 2 * half] = every(
            folded, line, pairs, lines
        ).astype(BF16)
    label = jnp.broadcast_to(class_ref[...].astype(F32), (8, pairs))
    info = flipped(jnp.concatenate([interp_ref[...].astype(F32), label], axis=0))
    out_ref[:, lines * 2 * half :] = info[:pairs].astype(BF16)


def fold(projections, interp_weights, pair_class):
    pairs, lines, width = projections.shape
    taps = interp_weights.transpose(1, 2, 0).reshape(-1, pairs)
    return pl.pallas_call(
        fold_kernel,
        out_shape=jax.ShapeDtypeStruct((pairs, lines * width // 2 + 128), BF16),
        scratch_shapes=[pltpu.VMEM((width // 256, pairs * lines, 128), F32)],
        compiler_params=vmem(12),
        name="fold_projections",
    )(projections.reshape(pairs * lines, width), taps, pair_class[None, :])


def sort_kernel(reach, count, capacity, pairs, *refs):
    x_hbm, owner_hbm, pair_hbm, shift_hbm, defocus_hbm = refs[:5]
    *outs, x_ref, owner_ref, pair_ref, shift_ref, defocus_ref, wide, sorted_ref, in_sem, out_sem = refs[5:]
    hbm = (owner_hbm, pair_hbm, shift_hbm, defocus_hbm, x_hbm)
    local = (owner_ref, pair_ref, shift_ref, defocus_ref, x_ref)
    loads = [pltpu.make_async_copy(a, b, in_sem.at[i]) for i, (a, b) in enumerate(zip(hbm, local))]
    for load in loads:
        load.start()
    particles = owner_ref.shape[1]
    length = x_ref.shape[1]
    lines = x_ref.shape[0] // particles
    slots = sorted_ref.shape[0]
    each = slots // len(outs)
    row = lax.broadcasted_iota(jnp.int32, (particles, particles), 0)
    column = lax.broadcasted_iota(jnp.int32, (particles, particles), 1)
    before = jnp.where(row < column, 1.0, 0.0).astype(BF16)
    for load in loads[:4]:
        load.wait()
    me = lax.axis_index("owner")
    owner = owner_ref[...]
    bins = owner & (count - 1)
    if len(outs) > 1:
        bins = bins ^ (me & (count - 1))
    step = ((me >> (count.bit_length() - 1)) - (owner >> (count.bit_length() - 1))) & (reach - 1)
    pair = step * pairs + pair_ref[...]
    padded = -(-count // 8) * 8
    hits = lax.broadcasted_iota(jnp.int32, (padded, particles), 0) == bins
    earlier = jnp.dot(jnp.where(hits, 1.0, 0.0).astype(BF16), before, preferred_element_type=F32)
    earlier = jnp.sum(jnp.where(hits, earlier, 0.0), axis=0, keepdims=True)
    place = bins * capacity + earlier.astype(jnp.int32)
    pick = lax.broadcasted_iota(jnp.int32, (slots, particles), 0) == place
    pick = jnp.where(pick, 1.0, 0.0).astype(BF16)
    kind = lax.broadcasted_iota(jnp.int32, (8, particles), 0)
    facts = jnp.where(kind == 0, defocus_ref[...].astype(F32), jnp.ones((8, particles), F32))
    facts = jnp.where(kind == 1, pair.astype(F32), facts)
    facts = jnp.where(kind == 2, shift_ref[...].astype(F32), facts)
    picked = jnp.dot(pick, flipped(facts).astype(BF16), preferred_element_type=F32)
    sorted_ref[:, lines * length :] = picked.astype(BF16)
    loads[4].wait()
    put_tiles(wide, x_ref[...].astype(F32))
    groups = out_sem.shape[1]
    stores = []
    for line in range(lines):
        rows = every(wide, line, particles, lines).astype(BF16)
        picked = jnp.dot(pick, rows, preferred_element_type=F32)
        sorted_ref[:, line * length : (line + 1) * length] = picked.astype(BF16)
        if (line + 1) % (lines // groups) == 0:
            group = line * groups // lines
            wide_group = lines // groups * length
            end = (group + 1) * wide_group + (128 if line == lines - 1 else 0)
            for j, out in enumerate(outs):
                stores.append(
                    pltpu.make_async_copy(
                        sorted_ref.at[j * each : (j + 1) * each, group * wide_group : end],
                        out.at[:, group * wide_group : end],
                        out_sem.at[j, group],
                    )
                )
                stores[-1].start()
    for store in stores:
        store.wait()


def sort_particles(images, owner, pair, shift, defocus, reach, count, capacity, pairs, pieces):
    particles, lines, length = images.shape
    slots = count * capacity
    each, width, groups = slots // pieces, lines * length + 128, 4
    args = [images.reshape(particles * lines, length)] + [a[None, :] for a in (owner, pair, shift, defocus)]
    return pl.pallas_call(
        lambda *refs: sort_kernel(reach, count, capacity, pairs, *refs),
        in_specs=[HBM] * 5,
        out_specs=[HBM] * pieces,
        out_shape=[jax.ShapeDtypeStruct((each, width), BF16)] * pieces,
        scratch_shapes=[pltpu.VMEM(a.shape, a.dtype) for a in args]
        + [
            pltpu.VMEM((length // 128, particles * lines, 128), F32),
            pltpu.VMEM((slots, width), BF16),
            pltpu.SemaphoreType.DMA((5,)),
            pltpu.SemaphoreType.DMA((pieces, groups)),
        ],
        compiler_params=vmem(20),
        name="sort_particles",
    )(*args)


def joined(refs, sizes, at):
    blocks, start = [], 0
    for size in sizes:
        block = refs[start][:, at]
        for ref in refs[start + 1 : start + size]:
            block = block + ref[:, at]
        blocks.append(block)
        start += size
    return jnp.concatenate(blocks, axis=0)


def score_kernel(scale, n_start, n_images, sizes, slab_lines, *refs):
    n_refs = sum(sizes)
    starts, refs = refs[:n_start], refs[n_start:]
    images, refs = refs[:n_images], refs[n_images:]
    facts_refs, refs = refs[:n_images], refs[n_images:]
    blocks, refs = refs[:n_refs], refs[n_refs:]
    infos, refs = refs[:n_refs], refs[n_refs:]
    table_ref, out_ref, aligned, scores, taps, spread, facts, cosine, cosine_imag, sine, power = refs
    step = pl.program_id(0)
    particles, half = cosine.shape
    pairs, slots = scores.shape
    rows = out_ref.shape[0]
    length = 2 * half
    lines = aligned.shape[0]
    here = images[0].shape[1] // length

    def chosen():
        pair = facts[1:2, :].astype(jnp.int32)
        return lax.broadcasted_iota(jnp.int32, (pairs, slots), 0) == pair

    @pl.when(step == 0)
    def _():
        found = jnp.concatenate([ref[...] for ref in facts_refs], axis=0).astype(F32)
        column = lax.broadcasted_iota(jnp.int32, (particles, half + 128), 1)
        folded = column.astype(F32) * (1.0 / length)
        ctf = -sine_of(found[:, :1] * 1500.0 * (folded * folded) + 0.2)
        shift = found[:, 2:3].astype(jnp.int32)
        turn = (shift * column[:, :half]) & (length - 1)
        turn = jnp.where(turn >= half, turn - length, turn).astype(F32) * (2.0 * math.pi / length)
        size = jnp.abs(turn)
        mirrored = jnp.where(size > 0.5 * math.pi, math.pi - size, size)
        swing = short_sine(jnp.where(turn < 0, -mirrored, mirrored))
        along = ctf[:, :half] * short_sine(0.5 * math.pi - size)
        nyquist = ctf[:, half : half + 1] * (1 - 2 * (shift & 1)).astype(F32)
        cosine[...] = along
        cosine_imag[...] = jnp.where(column[:, :half] == 0, nyquist, along)
        sine[...] = ctf[:, :half] * swing
        square = jnp.where(column <= half, ctf * ctf, 0.0)
        if particles < slots:
            square = jnp.concatenate([square, jnp.zeros((slots - particles, half + 128), F32)], axis=0)
            found = jnp.concatenate([found, jnp.zeros((slots - particles, 128), F32)], axis=0)
        power[...] = square.astype(BF16)
        for t in range(slots // 128):
            facts[:, t * 128 : (t + 1) * 128] = found[t * 128 : (t + 1) * 128].T[:8]
        scores[...] = jnp.zeros(scores.shape, F32)
        onehot = jnp.where(chosen(), 1.0, 0.0).astype(BF16)
        info = joined(infos, sizes, slice(None))
        tap = lax.dot_general(info, onehot, (((0,), (0,)), ((), ())), preferred_element_type=F32)
        put_tiles(taps, tap)
        label = tap[slab_lines * lines : slab_lines * lines + 1, :].astype(jnp.int32)
        group = lax.broadcasted_iota(jnp.int32, (rows, slots), 0) // (rows // CLASSES)
        spread[...] = jnp.where(group == label, 1.0, 0.0)

    total = scores[...]
    for i in range(here):
        at = slice(i * length, (i + 1) * length)
        lines_in = jnp.concatenate([ref[:, at] for ref in images], axis=0)
        spectra = jnp.dot(lines_in, table_ref[...], preferred_element_type=F32)
        spectra = spectra.astype(BF16).astype(F32)
        real, imag = spectra[:, :half], spectra[:, half:]
        turned = jnp.concatenate(
            [cosine[...] * real + sine[...] * imag, cosine_imag[...] * imag - sine[...] * real],
            axis=1,
        )
        if particles < slots:
            empty = jnp.zeros((slots - particles, length), F32)
            turned = jnp.concatenate([turned, empty], axis=0)
        aligned[step * here + i] = turned
        against = joined(blocks, sizes, at)
        total = total + lax.dot_general(
            against, turned.astype(BF16), (((1,), (1,)), ((), ())), preferred_element_type=F32
        )
    scores[...] = total

    @pl.when(step == pl.num_programs(0) - 1)
    def _():
        score = jnp.sum(jnp.where(chosen(), scores[...], 0.0), axis=0, keepdims=True)
        weight = facts[3:4, :] / (1.0 + jnp.exp(score * (-2.0 * scale)))
        upright = jnp.broadcast_to(weight, (128, slots)).T
        upright = jnp.concatenate([upright] * (length // 128), axis=1)
        slab = starts[0][:, :length] if starts else jnp.zeros((rows, length), F32)
        tap_sum = jnp.zeros((slab_lines, slots), F32)
        mask = spread[...].reshape(rows // 8, 8, slots)
        for line in range(lines):
            tap = every(taps, line, slab_lines, lines)
            tap_sum = tap_sum + tap
            tap = jnp.concatenate([tap] * (8 // slab_lines), axis=0)
            mixer = (mask * tap[None]).reshape(rows, slots).astype(BF16)
            contrib = (upright * aligned[line]).astype(BF16)
            slab = slab + jnp.dot(mixer, contrib, preferred_element_type=F32)
        tap = jnp.concatenate([tap_sum * weight] * (8 // slab_lines), axis=0)
        mixer = (mask * tap[None]).reshape(rows, slots).astype(BF16)
        powers = jnp.dot(mixer, power[...], preferred_element_type=F32)
        if starts:
            powers = powers + starts[0][:, length:]
        out_ref[:, :length] = slab.astype(out_ref.dtype)
        out_ref[:, length:] = powers.astype(out_ref.dtype)


def score_and_spread(start, images, references, rows, slab_lines, lines, length, dtype):
    half = length // 2
    particles = sum(a.shape[0] for a in images)
    slots = -(-particles // 128) * 128
    pairs = sum(a[0].shape[0] for a in references)
    sizes = [len(a) for a in references]
    references = [a for blocks in references for a in blocks]
    here = 4
    whole = lambda a: pl.BlockSpec(a.shape, lambda r: (0,) * a.ndim)
    line = lambda a: pl.BlockSpec((a.shape[0], here * length), lambda r: (0, r))
    info = lambda a: pl.BlockSpec((a.shape[0], 128), lambda r: (0, lines * length // 128))
    table = packed_table(length)
    width = length + half + 128
    return pl.pallas_call(
        lambda *refs: score_kernel(
            1.0 / math.sqrt(lines * length), len(start), len(images), sizes, slab_lines, *refs
        ),
        grid=(lines // here,),
        in_specs=[whole(a) for a in start]
        + [line(a) for a in images] + [info(a) for a in images]
        + [line(a) for a in references] + [info(a) for a in references] + [whole(table)],
        out_specs=pl.BlockSpec((rows, width), lambda r: (0, 0)),
        out_shape=jax.ShapeDtypeStruct((rows, width), dtype),
        scratch_shapes=[
            pltpu.VMEM((lines, slots, length), F32),
            pltpu.VMEM((pairs, slots), F32),
            pltpu.VMEM((slots // 128, 128, 128), F32),
            pltpu.VMEM((rows, slots), F32),
            pltpu.VMEM((8, slots), F32),
            pltpu.VMEM((particles, half), F32),
            pltpu.VMEM((particles, half), F32),
            pltpu.VMEM((particles, half), F32),
            pltpu.VMEM((slots, half + 128), BF16),
        ],
        compiler_params=vmem(36),
        name="score_and_spread",
    )(*start, *images, *images, *references, *references, table)


def finish_kernel(scale, x_ref, slab_ref, weights_ref):
    half = weights_ref.shape[1] // 2
    total = jnp.sum(x_ref[...].astype(F32), axis=0)
    flip = mirror(half)

    def mirrored(part):
        out = jnp.zeros(part.shape, F32)
        for _ in range(3):
            piece = part.astype(BF16)
            out = out + jnp.dot(piece, flip, preferred_element_type=F32)
            part = part - piece.astype(F32)
        return out

    real, imag, power = total[:, :half], total[:, half : 2 * half], total[:, 2 * half : 3 * half] * scale
    first = lax.broadcasted_iota(jnp.int32, real.shape, 1) == 0
    slab_ref[:, :half] = real
    slab_ref[:, half : 2 * half] = jnp.where(first, imag[:, :1], mirrored(real))
    slab_ref[:, 2 * half : 3 * half] = jnp.where(first, 0.0, imag)
    slab_ref[:, 3 * half :] = jnp.where(first, 0.0, -mirrored(imag))
    weights_ref[:, :half] = power
    weights_ref[:, half:] = jnp.where(first, total[:, 3 * half : 3 * half + 1] * scale, mirrored(power))


def finish(received, length, scale):
    rows = received.shape[1]
    return pl.pallas_call(
        lambda *refs: finish_kernel(scale, *refs),
        out_shape=(
            jax.ShapeDtypeStruct((rows, 2 * length), F32),
            jax.ShapeDtypeStruct((rows, length), F32),
        ),
        name="finish_slab",
    )(received)


def gather_rows(block, owners, reach, count):
    turn = lambda i: lax.ppermute(block, "owner", [(k, (k + i * count) % owners) for k in range(owners)])
    if reach != 4:
        return [(block,)] + [(turn(i),) for i in range(1, reach)]
    back, ahead = turn(1), turn(3)
    inner = range(count, 3 * count)
    up = lax.ppermute(back, "owner", [(k, k + count) for k in inner])
    down = lax.ppermute(ahead, "owner", [(k, k - count) for k in inner])
    return [(block,), (back,), (up, down), (ahead,)]


def on_device(
    images, defocus, owner_of, pair_of, shift_of, projections, interp_weights, pair_class
):
    particles, lines, length = images.shape
    owners = lax.axis_size("owner")
    capacity = 2 * particles // owners
    pairs, slab_lines, _ = interp_weights.shape
    rows = CLASSES * slab_lines
    reach = max(1, capacity // 4)
    count = owners // reach
    pieces = count if reach > 1 else 1
    moved = sort_particles(
        images, owner_of[:, 0], pair_of, shift_of, defocus, reach, count, reach * capacity, pairs, pieces
    )
    references = gather_rows(fold(projections, interp_weights, pair_class), owners, reach, count)
    sizes = (rows, slab_lines, lines, length)
    if reach > 1:
        swap = lambda a, i: lax.ppermute(a, "owner", [(k, k ^ i) for k in range(owners)]) if i else a
        arrived = [swap(a, i) for i, a in enumerate(moved)]
        partial = score_and_spread([], arrived[:-1], references, *sizes, F32)
        partial = score_and_spread([partial], arrived[-1:], references, *sizes, BF16)
    else:
        arrived = lax.all_to_all(moved[0], "owner", split_axis=0, concat_axis=0, tiled=True)
        partial = score_and_spread([], [arrived], references, *sizes, BF16)
    received = lax.all_to_all(partial, "owner", split_axis=0, concat_axis=0, tiled=True)
    return finish(
        received.reshape(owners, rows // owners, -1), length, CLASSES / (particles * owners)
    )


def solution(mesh):
    return jax.shard_map(
        on_device,
        mesh=mesh,
        in_specs=(
            P(("half", "owner"), None, None),
            P(("half", "owner")),
            P(("half", "owner"), None),
            P(("half", "owner")),
            P(("half", "owner")),
            P(("half", "owner"), None, None),
            P(("half", "owner"), None, None),
            P(("half", "owner")),
        ),
        out_specs=(P(("half", "owner"), None), P(("half", "owner"), None)),
        check_vma=False,
    )
```

```python
import math

import jax
import jax.numpy as jnp
import numpy as np
from jax import lax
from jax.experimental import pallas as pl
from jax.experimental.pallas import tpu as pltpu
from jax.sharding import PartitionSpec as P

CLASSES = 64
F32 = jnp.float32
BF16 = jnp.bfloat16
HBM = pl.BlockSpec(memory_space=pltpu.MemorySpace.HBM)


def vmem(megabytes):
    return pltpu.CompilerParams(vmem_limit_bytes=megabytes * 1024 * 1024)


def packed_table(length):
    half = length // 2
    product = np.arange(length)[:, None] * np.arange(half + 1)[None, :] % length
    angles = product * (2.0 * math.pi / length)
    cosine, sine = np.cos(angles), -np.sin(angles)
    sine[:, 0] = cosine[:, half]
    table = np.concatenate([cosine[:, :half], sine[:, :half]], axis=1) / math.sqrt(length)
    return jnp.asarray(table, F32).astype(BF16)


def mirror(half):
    row = lax.broadcasted_iota(jnp.int32, (half, half), 0)
    column = lax.broadcasted_iota(jnp.int32, (half, half), 1)
    return jnp.where(row + column == half, 1.0, 0.0).astype(BF16)


def put_tiles(ref, values):
    for t in range(ref.shape[0]):
        ref[t] = values[:, t * 128 : (t + 1) * 128]


def every(ref, start, count, stride):
    picked = [ref[t, pl.ds(start, count, stride=stride), :] for t in range(ref.shape[0])]
    return jnp.concatenate(picked, axis=1)


def flipped(rows):
    down, across = rows.shape
    if across < 128:
        rows = jnp.concatenate([rows, jnp.zeros((down, 128 - across), F32)], axis=1)
    if down < 128:
        rows = jnp.concatenate([rows, jnp.zeros((128 - down, 128), F32)], axis=0)
    return rows.T


def short_sine(x):
    square = x * x
    total = jnp.full(x.shape, -1.0 / 39916800.0, F32)
    for factor in (1.0 / 362880.0, -1.0 / 5040.0, 1.0 / 120.0, -1.0 / 6.0, 1.0):
        total = total * square + factor
    return total * x


def sine_of(x):
    turns = jnp.floor(x * (0.5 / math.pi) + 0.5)
    x = ((x - turns * 6.28125) - turns * 0.0019340515136718750) - turns * 1.2556659145e-06
    x = jnp.where(x > 0.5 * math.pi, math.pi - x, jnp.where(x < -0.5 * math.pi, -math.pi - x, x))
    return short_sine(x)


def fold_kernel(x_ref, interp_ref, class_ref, out_ref, folded):
    pairs, width = out_ref.shape
    half = x_ref.shape[1] // 4
    lines = x_ref.shape[0] // pairs
    flip = mirror(half)
    real_low, real_high = x_ref[:, :half], x_ref[:, half : 2 * half]
    imag_low, imag_high = x_ref[:, 2 * half : 3 * half], x_ref[:, 3 * half :]
    real = real_low.astype(F32) + jnp.dot(real_high, flip, preferred_element_type=F32)
    imag = imag_low.astype(F32) - jnp.dot(imag_high, flip, preferred_element_type=F32)
    lane = lax.broadcasted_iota(jnp.int32, imag.shape, 1)
    imag = jnp.where(lane == 0, real_high.astype(F32)[:, :1], imag)
    put_tiles(folded, jnp.concatenate([real, imag], axis=1))
    for line in range(lines):
        out_ref[:, line * 2 * half : (line + 1) * 2 * half] = every(
            folded, line, pairs, lines
        ).astype(BF16)
    label = jnp.broadcast_to(class_ref[...].astype(F32), (8, pairs))
    info = flipped(jnp.concatenate([interp_ref[...].astype(F32), label], axis=0))
    out_ref[:, lines * 2 * half :] = info[:pairs].astype(BF16)


def fold(projections, interp_weights, pair_class):
    pairs, lines, width = projections.shape
    taps = interp_weights.transpose(1, 2, 0).reshape(-1, pairs)
    return pl.pallas_call(
        fold_kernel,
        out_shape=jax.ShapeDtypeStruct((pairs, lines * width // 2 + 128), BF16),
        scratch_shapes=[pltpu.VMEM((width // 256, pairs * lines, 128), F32)],
        compiler_params=vmem(12),
        name="fold_projections",
    )(projections.reshape(pairs * lines, width), taps, pair_class[None, :])


def sort_kernel(reach, count, capacity, pairs, *refs):
    x_hbm, owner_hbm, pair_hbm, shift_hbm, defocus_hbm = refs[:5]
    *outs, x_ref, owner_ref, pair_ref, shift_ref, defocus_ref, wide, sorted_ref, in_sem, out_sem = refs[5:]
    hbm = (owner_hbm, pair_hbm, shift_hbm, defocus_hbm, x_hbm)
    local = (owner_ref, pair_ref, shift_ref, defocus_ref, x_ref)
    loads = [pltpu.make_async_copy(a, b, in_sem.at[i]) for i, (a, b) in enumerate(zip(hbm, local))]
    for load in loads:
        load.start()
    particles = owner_ref.shape[1]
    length = x_ref.shape[1]
    lines = x_ref.shape[0] // particles
    slots = sorted_ref.shape[0]
    each = slots // len(outs)
    row = lax.broadcasted_iota(jnp.int32, (particles, particles), 0)
    column = lax.broadcasted_iota(jnp.int32, (particles, particles), 1)
    before = jnp.where(row < column, 1.0, 0.0).astype(BF16)
    for load in loads[:4]:
        load.wait()
    me = lax.axis_index("owner")
    owner = owner_ref[...]
    bins = owner & (count - 1)
    if len(outs) > 1:
        bins = bins ^ (me & (count - 1))
    step = ((me >> (count.bit_length() - 1)) - (owner >> (count.bit_length() - 1))) & (reach - 1)
    pair = step * pairs + pair_ref[...]
    padded = -(-count // 8) * 8
    hits = lax.broadcasted_iota(jnp.int32, (padded, particles), 0) == bins
    earlier = jnp.dot(jnp.where(hits, 1.0, 0.0).astype(BF16), before, preferred_element_type=F32)
    earlier = jnp.sum(jnp.where(hits, earlier, 0.0), axis=0, keepdims=True)
    place = bins * capacity + earlier.astype(jnp.int32)
    pick = lax.broadcasted_iota(jnp.int32, (slots, particles), 0) == place
    pick = jnp.where(pick, 1.0, 0.0).astype(BF16)
    kind = lax.broadcasted_iota(jnp.int32, (8, particles), 0)
    facts = jnp.where(kind == 0, defocus_ref[...].astype(F32), jnp.ones((8, particles), F32))
    facts = jnp.where(kind == 1, pair.astype(F32), facts)
    facts = jnp.where(kind == 2, shift_ref[...].astype(F32), facts)
    picked = jnp.dot(pick, flipped(facts).astype(BF16), preferred_element_type=F32)
    sorted_ref[:, lines * length :] = picked.astype(BF16)
    loads[4].wait()
    put_tiles(wide, x_ref[...].astype(F32))
    groups = out_sem.shape[1]
    stores = []
    for line in range(lines):
        rows = every(wide, line, particles, lines).astype(BF16)
        picked = jnp.dot(pick, rows, preferred_element_type=F32)
        sorted_ref[:, line * length : (line + 1) * length] = picked.astype(BF16)
        if (line + 1) % (lines // groups) == 0:
            group = line * groups // lines
            wide_group = lines // groups * length
            end = (group + 1) * wide_group + (128 if line == lines - 1 else 0)
            for j, out in enumerate(outs):
                stores.append(
                    pltpu.make_async_copy(
                        sorted_ref.at[j * each : (j + 1) * each, group * wide_group : end],
                        out.at[:, group * wide_group : end],
                        out_sem.at[j, group],
                    )
                )
                stores[-1].start()
    for store in stores:
        store.wait()


def sort_particles(images, owner, pair, shift, defocus, reach, count, capacity, pairs, pieces):
    particles, lines, length = images.shape
    slots = count * capacity
    each, width, groups = slots // pieces, lines * length + 128, 4
    args = [images.reshape(particles * lines, length)] + [a[None, :] for a in (owner, pair, shift, defocus)]
    return pl.pallas_call(
        lambda *refs: sort_kernel(reach, count, capacity, pairs, *refs),
        in_specs=[HBM] * 5,
        out_specs=[HBM] * pieces,
        out_shape=[jax.ShapeDtypeStruct((each, width), BF16)] * pieces,
        scratch_shapes=[pltpu.VMEM(a.shape, a.dtype) for a in args]
        + [
            pltpu.VMEM((length // 128, particles * lines, 128), F32),
            pltpu.VMEM((slots, width), BF16),
            pltpu.SemaphoreType.DMA((5,)),
            pltpu.SemaphoreType.DMA((pieces, groups)),
        ],
        compiler_params=vmem(60),
        name="sort_particles",
    )(*args)


def joined(blocks, at):
    return jnp.concatenate([sum((ref[:, at] for ref in block[1:]), block[0][:, at]) for block in blocks], axis=0)


def score_kernel(scale, n_images, sizes, slab_lines, lines, *refs):
    images, refs = refs[:n_images], refs[n_images:]
    blocks = []
    for size in sizes:
        blocks.append(refs[:size])
        refs = refs[size:]
    table_ref, out_ref, aligned, taps, cosine, cosine_imag, sine, tap_mask = refs
    slots, half = cosine.shape
    length = 2 * half
    rows = out_ref.shape[0]
    extra = slice(lines * length, lines * length + 128)
    info = joined(blocks, extra)
    pairs = info.shape[0]

    found = jnp.concatenate([ref[:, extra] for ref in images], axis=0).astype(F32)
    column = lax.broadcasted_iota(jnp.int32, (slots, half + 128), 1)
    folded = column.astype(F32) * (1.0 / length)
    ctf = -sine_of(found[:, :1] * 1500.0 * (folded * folded) + 0.2)
    shift = found[:, 2:3].astype(jnp.int32)
    turn = (shift * column[:, :half]) & (length - 1)
    turn = jnp.where(turn >= half, turn - length, turn).astype(F32) * (2.0 * math.pi / length)
    size = jnp.abs(turn)
    mirrored = jnp.where(size > 0.5 * math.pi, math.pi - size, size)
    swing = short_sine(jnp.where(turn < 0, -mirrored, mirrored))
    along = ctf[:, :half] * short_sine(0.5 * math.pi - size)
    nyquist = ctf[:, half : half + 1] * (1 - 2 * (shift & 1)).astype(F32)
    cosine[...] = along
    cosine_imag[...] = jnp.where(column[:, :half] == 0, nyquist, along)
    sine[...] = ctf[:, :half] * swing
    power = jnp.where(column <= half, ctf * ctf, 0.0)

    pair_row = jnp.concatenate(
        [found[t : t + 128].T[1:2] for t in range(0, slots, 128)], axis=1
    ).astype(jnp.int32)
    onehot = lax.broadcasted_iota(jnp.int32, (pairs, slots), 0) == pair_row
    onehot = jnp.where(onehot, 1.0, 0.0).astype(BF16)
    tap = lax.dot_general(info, onehot, (((0,), (0,)), ((), ())), preferred_element_type=F32)
    put_tiles(taps, tap)
    label = tap[slab_lines * lines : slab_lines * lines + 1, :].astype(jnp.int32)
    group = lax.broadcasted_iota(jnp.int32, (rows, slots), 0) // (rows // CLASSES)
    tap_mask[...] = jnp.where(group == label, 1.0, 0.0)

    here = 4
    scores = jnp.zeros((slots, pairs), F32)
    for first in range(0, lines, here):
        at = [slice((first + i) * length, (first + i + 1) * length) for i in range(here)]
        lines_in = jnp.concatenate([ref[:, cut] for cut in at for ref in images], axis=0)
        spectra = jnp.dot(lines_in, table_ref[...], preferred_element_type=F32)
        spectra = spectra.astype(BF16).astype(F32)
        turns = []
        for i in range(here):
            real = spectra[i * slots : (i + 1) * slots, :half]
            imag = spectra[i * slots : (i + 1) * slots, half:]
            turned = jnp.concatenate(
                [cosine[...] * real + sine[...] * imag, cosine_imag[...] * imag - sine[...] * real],
                axis=1,
            )
            aligned[first + i] = turned
            turns.append(turned.astype(BF16))
        against = joined(blocks, slice(first * length, (first + here) * length))
        scores = scores + lax.dot_general(
            jnp.concatenate(turns, axis=1), against, (((1,), (1,)), ((), ())),
            preferred_element_type=F32,
        )

    chosen = lax.broadcasted_iota(jnp.int32, (slots, pairs), 1) == found[:, 1:2].astype(jnp.int32)
    score = jnp.sum(jnp.where(chosen, scores, 0.0), axis=1, keepdims=True)
    weight = found[:, 3:4] / (1.0 + jnp.exp(score * (-2.0 * scale)))
    slab = jnp.zeros((rows, length), F32)
    tap_sum = jnp.zeros((slab_lines, slots), F32)

    def mixer(tap):
        tap = jnp.concatenate([tap] * (8 // slab_lines), axis=0)
        mask = tap_mask[...].reshape(rows // 8, 8, slots)
        return (mask * tap[None]).reshape(rows, slots).astype(BF16)

    for line in range(lines):
        tap = every(taps, line, slab_lines, lines)
        tap_sum = tap_sum + tap
        contrib = (weight * aligned[line]).astype(BF16)
        slab = slab + jnp.dot(mixer(tap), contrib, preferred_element_type=F32)
    out_ref[:, :length] = slab.astype(BF16)
    powers = jnp.dot(mixer(tap_sum), (weight * power).astype(BF16), preferred_element_type=F32)
    out_ref[:, length:] = powers.astype(BF16)


def score_and_spread(images, references, rows, slab_lines, lines, length):
    half = length // 2
    slots = sum(a.shape[0] for a in images)
    sizes = [len(a) for a in references]
    references = [a for blocks in references for a in blocks]
    width = length + half + 128
    return pl.pallas_call(
        lambda *refs: score_kernel(
            1.0 / math.sqrt(lines * length), len(images), sizes, slab_lines, lines, *refs
        ),
        out_shape=jax.ShapeDtypeStruct((rows, width), BF16),
        scratch_shapes=[
            pltpu.VMEM((lines, slots, length), F32),
            pltpu.VMEM((slots // 128, 128, 128), F32),
            pltpu.VMEM((slots, half), F32),
            pltpu.VMEM((slots, half), F32),
            pltpu.VMEM((slots, half), F32),
            pltpu.VMEM((rows, slots), F32),
        ],
        compiler_params=vmem(32),
        name="score_and_spread",
    )(*images, *references, packed_table(length))


def finish_kernel(scale, x_ref, slab_ref, weights_ref):
    half = weights_ref.shape[1] // 2
    total = jnp.sum(x_ref[...].astype(F32), axis=0)
    flip = mirror(half)

    def mirrored(part):
        out = jnp.zeros(part.shape, F32)
        for _ in range(3):
            piece = part.astype(BF16)
            out = out + jnp.dot(piece, flip, preferred_element_type=F32)
            part = part - piece.astype(F32)
        return out

    real, imag, power = total[:, :half], total[:, half : 2 * half], total[:, 2 * half : 3 * half] * scale
    first = lax.broadcasted_iota(jnp.int32, real.shape, 1) == 0
    slab_ref[:, :half] = real
    slab_ref[:, half : 2 * half] = jnp.where(first, imag[:, :1], mirrored(real))
    slab_ref[:, 2 * half : 3 * half] = jnp.where(first, 0.0, imag)
    slab_ref[:, 3 * half :] = jnp.where(first, 0.0, -mirrored(imag))
    weights_ref[:, :half] = power
    weights_ref[:, half:] = jnp.where(first, total[:, 3 * half : 3 * half + 1] * scale, mirrored(power))


def finish(received, length, scale):
    rows = received.shape[1]
    return pl.pallas_call(
        lambda *refs: finish_kernel(scale, *refs),
        out_shape=(
            jax.ShapeDtypeStruct((rows, 2 * length), F32),
            jax.ShapeDtypeStruct((rows, length), F32),
        ),
        name="finish_slab",
    )(received)


def gather_rows(block, owners, reach, count):
    turn = lambda i: lax.ppermute(block, "owner", [(k, (k + i * count) % owners) for k in range(owners)])
    if reach != 4:
        return [(block,)] + [(turn(i),) for i in range(1, reach)]
    back, ahead = turn(1), turn(3)
    inner = range(count, 3 * count)
    up = lax.ppermute(back, "owner", [(k, k + count) for k in inner])
    down = lax.ppermute(ahead, "owner", [(k, k - count) for k in inner])
    return [(block,), (back,), (up, down), (ahead,)]


def on_device(
    images, defocus, owner_of, pair_of, shift_of, projections, interp_weights, pair_class
):
    particles, lines, length = images.shape
    owners = lax.axis_size("owner")
    capacity = 2 * particles // owners
    pairs, slab_lines, _ = interp_weights.shape
    rows = CLASSES * slab_lines
    reach = max(1, capacity // 4)
    count = owners // reach
    pieces = count if reach > 1 else 1
    moved = sort_particles(
        images, owner_of[:, 0], pair_of, shift_of, defocus, reach, count, reach * capacity, pairs, pieces
    )
    references = gather_rows(fold(projections, interp_weights, pair_class), owners, reach, count)
    if reach > 1:
        swap = lambda a, i: lax.ppermute(a, "owner", [(k, k ^ i) for k in range(owners)]) if i else a
        arrived = [swap(a, i) for i, a in enumerate(moved)]
    else:
        arrived = [lax.all_to_all(moved[0], "owner", split_axis=0, concat_axis=0, tiled=True)]
    partial = score_and_spread(arrived, references, rows, slab_lines, lines, length)
    received = lax.all_to_all(partial, "owner", split_axis=0, concat_axis=0, tiled=True)
    return finish(
        received.reshape(owners, rows // owners, -1), length, CLASSES / (particles * owners)
    )


def solution(mesh):
    return jax.shard_map(
        on_device,
        mesh=mesh,
        in_specs=(
            P(("half", "owner"), None, None),
            P(("half", "owner")),
            P(("half", "owner"), None),
            P(("half", "owner")),
            P(("half", "owner")),
            P(("half", "owner"), None, None),
            P(("half", "owner"), None, None),
            P(("half", "owner")),
        ),
        out_specs=(P(("half", "owner"), None), P(("half", "owner"), None)),
        check_vma=False,
    )
```

```python
import math

import jax
import jax.numpy as jnp
import numpy as np
from jax import lax
from jax.experimental import pallas as pl
from jax.experimental.pallas import tpu as pltpu
from jax.sharding import PartitionSpec as P

CLASSES = 64
LEVELS = 256
F32 = jnp.float32
BF16 = jnp.bfloat16
HBM = pl.BlockSpec(memory_space=pltpu.MemorySpace.HBM)


def vmem(megabytes):
    return pltpu.CompilerParams(vmem_limit_bytes=megabytes * 1024 * 1024)


def packed_table(length):
    half = length // 2
    product = np.arange(length)[:, None] * np.arange(half + 1)[None, :] % length
    angles = product * (2.0 * math.pi / length)
    cosine, sine = np.cos(angles), -np.sin(angles)
    sine[:, 0] = cosine[:, half]
    table = np.concatenate([cosine[:, :half], sine[:, :half]], axis=1) / math.sqrt(length)
    return jnp.asarray(table, F32).astype(BF16)


def mirror(half):
    row = lax.broadcasted_iota(jnp.int32, (half, half), 0)
    column = lax.broadcasted_iota(jnp.int32, (half, half), 1)
    return jnp.where(row + column == half, 1.0, 0.0).astype(BF16)


def put_tiles(ref, values):
    for t in range(ref.shape[0]):
        ref[t] = values[:, t * 128 : (t + 1) * 128]


def every(ref, start, count, stride):
    picked = [ref[t, pl.ds(start, count, stride=stride), :] for t in range(ref.shape[0])]
    return jnp.concatenate(picked, axis=1)


def flipped(rows):
    down, across = rows.shape
    if across < 128:
        rows = jnp.concatenate([rows, jnp.zeros((down, 128 - across), F32)], axis=1)
    if down < 128:
        rows = jnp.concatenate([rows, jnp.zeros((128 - down, 128), F32)], axis=0)
    return rows.T


def short_sine(x):
    square = x * x
    total = jnp.full(x.shape, -1.0 / 39916800.0, F32)
    for factor in (1.0 / 362880.0, -1.0 / 5040.0, 1.0 / 120.0, -1.0 / 6.0, 1.0):
        total = total * square + factor
    return total * x


def sine_of(x):
    turns = jnp.floor(x * (0.5 / math.pi) + 0.5)
    x = ((x - turns * 6.28125) - turns * 0.0019340515136718750) - turns * 1.2556659145e-06
    x = jnp.where(x > 0.5 * math.pi, math.pi - x, jnp.where(x < -0.5 * math.pi, -math.pi - x, x))
    return short_sine(x)


def fold_kernel(x_ref, interp_ref, class_ref, out_ref, folded):
    pairs, width = out_ref.shape
    half = x_ref.shape[1] // 4
    lines = x_ref.shape[0] // pairs
    flip = mirror(half)
    real_low, real_high = x_ref[:, :half], x_ref[:, half : 2 * half]
    imag_low, imag_high = x_ref[:, 2 * half : 3 * half], x_ref[:, 3 * half :]
    real = real_low.astype(F32) + jnp.dot(real_high, flip, preferred_element_type=F32)
    imag = imag_low.astype(F32) - jnp.dot(imag_high, flip, preferred_element_type=F32)
    lane = lax.broadcasted_iota(jnp.int32, imag.shape, 1)
    imag = jnp.where(lane == 0, real_high.astype(F32)[:, :1], imag)
    put_tiles(folded, jnp.concatenate([real, imag], axis=1))
    for line in range(lines):
        out_ref[:, line * 2 * half : (line + 1) * 2 * half] = every(
            folded, line, pairs, lines
        ).astype(BF16)
    label = jnp.broadcast_to(class_ref[...].astype(F32), (8, pairs))
    info = flipped(jnp.concatenate([interp_ref[...].astype(F32), label], axis=0))
    out_ref[:, lines * 2 * half :] = info[:pairs].astype(BF16)


def fold(projections, interp_weights, pair_class):
    pairs, lines, width = projections.shape
    taps = interp_weights.transpose(1, 2, 0).reshape(-1, pairs)
    return pl.pallas_call(
        fold_kernel,
        out_shape=jax.ShapeDtypeStruct((pairs, lines * width // 2 + 128), BF16),
        scratch_shapes=[pltpu.VMEM((width // 256, pairs * lines, 128), F32)],
        compiler_params=vmem(12),
        name="fold_projections",
    )(projections.reshape(pairs * lines, width), taps, pair_class[None, :])


def sort_kernel(reach, count, capacity, pairs, *refs):
    sources, refs = refs[:6], refs[6:]
    *outs, x_ref, owner_ref, pair_ref, shift_ref, defocus_ref, table_ref, wide, sorted_ref, in_sem, x_sem, out_sem = refs
    loads = [
        pltpu.make_async_copy(a, b, in_sem.at[i])
        for i, (a, b) in enumerate(
            zip(sources[1:], (owner_ref, pair_ref, shift_ref, defocus_ref, table_ref))
        )
    ]
    parts = x_sem.shape[0]
    share = x_ref.shape[0] // parts
    cuts = [slice(i * share, (i + 1) * share) for i in range(parts)]
    chunks = [
        pltpu.make_async_copy(sources[0].at[cut], x_ref.at[cut], x_sem.at[i])
        for i, cut in enumerate(cuts)
    ]
    for copy in loads + chunks:
        copy.start()
    particles = owner_ref.shape[1]
    length = x_ref.shape[1]
    half = length // 2
    lines = x_ref.shape[0] // particles
    slots = sorted_ref.shape[0]
    each = slots // len(outs)
    row = lax.broadcasted_iota(jnp.int32, (particles, particles), 0)
    column = lax.broadcasted_iota(jnp.int32, (particles, particles), 1)
    before = jnp.where(row < column, 1.0, 0.0).astype(BF16)
    for load in loads[:4]:
        load.wait()
    me = lax.axis_index("owner")
    owner = owner_ref[...]
    bins = owner & (count - 1)
    if len(outs) > 1:
        bins = bins ^ (me & (count - 1))
    step = ((me >> (count.bit_length() - 1)) - (owner >> (count.bit_length() - 1))) & (reach - 1)
    pair = step * pairs + pair_ref[...]
    padded = -(-count // 8) * 8
    hits = lax.broadcasted_iota(jnp.int32, (padded, particles), 0) == bins
    earlier = jnp.dot(jnp.where(hits, 1.0, 0.0).astype(BF16), before, preferred_element_type=F32)
    earlier = jnp.sum(jnp.where(hits, earlier, 0.0), axis=0, keepdims=True)
    place = bins * capacity + earlier.astype(jnp.int32)
    pick = lax.broadcasted_iota(jnp.int32, (slots, particles), 0) == place
    pick = jnp.where(pick, 1.0, 0.0).astype(BF16)
    defocus = defocus_ref[...].astype(F32)
    level = jnp.where(defocus < 2.0, (defocus - 1.0) * 128.0, 128.0 + (defocus - 2.0) * 64.0)
    kind = lax.broadcasted_iota(jnp.int32, (8, particles), 0)
    facts = jnp.where(kind == 0, jnp.floor(level + 0.5), jnp.ones((8, particles), F32))
    facts = jnp.where(kind == 1, pair.astype(F32), facts)
    facts = jnp.where(kind == 2, shift_ref[...].astype(F32), facts)
    facts = flipped(jnp.where(kind == 4, defocus, facts))
    picked = jnp.dot(pick, facts.astype(BF16), preferred_element_type=F32)
    sorted_ref[:, lines * length :] = picked.astype(BF16)

    column = lax.broadcasted_iota(jnp.int32, (particles, half + 128), 1)
    folded = column.astype(F32) * (1.0 / length)
    ctf = -sine_of(facts[:, 4:5] * 1500.0 * (folded * folded) + 0.2)
    shift = facts[:, 2:3].astype(jnp.int32)
    turn = (shift * column[:, :half]) & (length - 1)
    turn = jnp.where(turn >= half, turn - length, turn).astype(F32) * (2.0 * math.pi / length)
    size = jnp.abs(turn)
    mirrored = jnp.where(size > 0.5 * math.pi, math.pi - size, size)
    swing = short_sine(jnp.where(turn < 0, -mirrored, mirrored))
    cosine = ctf[:, :half] * short_sine(0.5 * math.pi - size)
    nyquist = ctf[:, half : half + 1] * (1 - 2 * (shift & 1)).astype(F32)
    cosine_imag = jnp.where(column[:, :half] == 0, nyquist, cosine)
    sine = ctf[:, :half] * swing

    loads[4].wait()
    for chunk, cut in zip(chunks, cuts):
        chunk.wait()
        spectra = jnp.dot(x_ref[cut], table_ref[...], preferred_element_type=F32)
        spectra = spectra.astype(BF16).astype(F32)
        for t in range(length // 128):
            wide[t, cut] = spectra[:, t * 128 : (t + 1) * 128]
    groups = out_sem.shape[1]
    stores = []
    for line in range(lines):
        spectra = every(wide, line, particles, lines)
        real, imag = spectra[:, :half], spectra[:, half:]
        turned = jnp.concatenate(
            [cosine * real + sine * imag, cosine_imag * imag - sine * real], axis=1
        )
        picked = jnp.dot(pick, turned.astype(BF16), preferred_element_type=F32)
        sorted_ref[:, line * length : (line + 1) * length] = picked.astype(BF16)
        if (line + 1) % (lines // groups) == 0:
            group = line * groups // lines
            wide_group = lines // groups * length
            end = (group + 1) * wide_group + (128 if line == lines - 1 else 0)
            for j, out in enumerate(outs):
                stores.append(
                    pltpu.make_async_copy(
                        sorted_ref.at[j * each : (j + 1) * each, group * wide_group : end],
                        out.at[:, group * wide_group : end],
                        out_sem.at[j, group],
                    )
                )
                stores[-1].start()
    for store in stores:
        store.wait()


def sort_particles(images, owner, pair, shift, defocus, reach, count, capacity, pairs, pieces):
    particles, lines, length = images.shape
    slots = count * capacity
    each, width, groups = slots // pieces, lines * length + 128, 4
    args = [images.reshape(particles * lines, length)] + [a[None, :] for a in (owner, pair, shift, defocus)]
    args.append(packed_table(length))
    return pl.pallas_call(
        lambda *refs: sort_kernel(reach, count, capacity, pairs, *refs),
        in_specs=[HBM] * 6,
        out_specs=[HBM] * pieces,
        out_shape=[jax.ShapeDtypeStruct((each, width), BF16)] * pieces,
        scratch_shapes=[pltpu.VMEM(a.shape, a.dtype) for a in args]
        + [
            pltpu.VMEM((length // 128, particles * lines, 128), F32),
            pltpu.VMEM((slots, width), BF16),
            pltpu.SemaphoreType.DMA((5,)),
            pltpu.SemaphoreType.DMA((4,)),
            pltpu.SemaphoreType.DMA((pieces, groups)),
        ],
        compiler_params=vmem(60),
        name="sort_particles",
    )(*args)


def joined(blocks, at):
    return jnp.concatenate([sum((ref[:, at] for ref in block[1:]), block[0][:, at]) for block in blocks], axis=0)


def score_kernel(scale, n_images, sizes, slab_lines, lines, length, *refs):
    images, refs = refs[:n_images], refs[n_images:]
    blocks = []
    for size in sizes:
        blocks.append(refs[:size])
        refs = refs[size:]
    out_ref, taps = refs
    info = joined(blocks, slice(lines * length, lines * length + 128))
    pairs, rows = info.shape[0], out_ref.shape[0]
    found = jnp.concatenate([ref[:, lines * length :] for ref in images], axis=0).astype(F32)
    slots = found.shape[0]
    here = 4

    def stacked(line):
        return jnp.concatenate(
            [ref[:, line * length : (line + 1) * length] for ref in images], axis=0
        )

    scores = jnp.zeros((slots, pairs), F32)
    for line in range(lines):
        block = joined(blocks, slice(line * length, (line + 1) * length))
        across = block.astype(F32).T.astype(BF16)
        scores = scores + jnp.dot(stacked(line), across, preferred_element_type=F32)

    pair_row = jnp.concatenate(
        [found[t : t + 128].T[1:2] for t in range(0, slots, 128)], axis=1
    ).astype(jnp.int32)
    onehot = lax.broadcasted_iota(jnp.int32, (pairs, slots), 0) == pair_row
    onehot = jnp.where(onehot, 1.0, 0.0).astype(BF16)
    tap = lax.dot_general(info, onehot, (((0,), (0,)), ((), ())), preferred_element_type=F32)
    put_tiles(taps, tap)
    label = tap[slab_lines * lines : slab_lines * lines + 1, :].astype(jnp.int32)
    group = lax.broadcasted_iota(jnp.int32, (rows, slots), 0) // (rows // CLASSES)
    mask = jnp.where(group == label, 1.0, 0.0).astype(BF16).reshape(rows // 16, 16, slots)

    def mixer(tap):
        tap = jnp.concatenate([tap] * (16 // slab_lines), axis=0).astype(BF16)
        return (mask * tap[None]).reshape(rows, slots)

    chosen = lax.broadcasted_iota(jnp.int32, (slots, pairs), 1) == found[:, 1:2].astype(jnp.int32)
    score = jnp.sum(jnp.where(chosen, scores, 0.0), axis=1, keepdims=True)
    weight = found[:, 3:4] / (1.0 + jnp.exp(score * (-2.0 * scale)))
    slab = jnp.zeros((rows, length), F32)
    tap_sum = jnp.zeros((slab_lines, slots), F32)
    for first in range(0, lines, here):
        mixers, contribs = [], []
        for line in range(first, first + here):
            tap = every(taps, line, slab_lines, lines)
            tap_sum = tap_sum + tap
            mixers.append(mixer(tap))
            contribs.append((weight * stacked(line).astype(F32)).astype(BF16))
        slab = slab + jnp.dot(
            jnp.concatenate(mixers, axis=1), jnp.concatenate(contribs, axis=0),
            preferred_element_type=F32,
        )
    out_ref[:, :length] = slab.astype(BF16)
    levels = lax.broadcasted_iota(jnp.int32, (slots, LEVELS), 1) == found[:, :1].astype(jnp.int32)
    levels = jnp.where(levels, weight, 0.0).astype(BF16)
    levels = jnp.dot(mixer(tap_sum), levels, preferred_element_type=F32)
    out_ref[:, length:] = levels.astype(BF16)


def score_and_spread(images, references, rows, slab_lines, lines, length):
    slots = sum(a.shape[0] for a in images)
    sizes = [len(a) for a in references]
    references = [a for blocks in references for a in blocks]
    return pl.pallas_call(
        lambda *refs: score_kernel(
            1.0 / math.sqrt(lines * length), len(images), sizes, slab_lines, lines, length, *refs
        ),
        out_shape=jax.ShapeDtypeStruct((rows, length + LEVELS), BF16),
        scratch_shapes=[pltpu.VMEM((slots // 128, 128, 128), F32)],
        compiler_params=vmem(24),
        name="score_and_spread",
    )(*images, *references)


def level_powers(length, scale):
    level = np.arange(LEVELS)
    defocus = np.where(level < 128, 1.0 + level / 128.0, 2.0 + (level - 128) / 64.0).astype(np.float32)
    column = np.arange(length)
    folded = np.minimum(column, length - column).astype(np.float32) / np.float32(length)
    phase = (defocus * np.float32(1500.0))[:, None] * (folded * folded)[None, :] + np.float32(0.2)
    powers = np.sin(phase.astype(np.float64)) ** 2 * scale
    return jnp.asarray(np.where(level[:, None] <= 192, powers, 0.0), F32)


def finish_kernel(x_ref, powers_ref, slab_ref, weights_ref):
    half = slab_ref.shape[1] // 4
    total = jnp.sum(x_ref[...].astype(F32), axis=0)
    flip = mirror(half)

    def mirrored(part):
        out = jnp.zeros(part.shape, F32)
        for _ in range(3):
            piece = part.astype(BF16)
            out = out + jnp.dot(piece, flip, preferred_element_type=F32)
            part = part - piece.astype(F32)
        return out

    real, imag = total[:, :half], total[:, half : 2 * half]
    first = lax.broadcasted_iota(jnp.int32, real.shape, 1) == 0
    slab_ref[:, :half] = real
    slab_ref[:, half : 2 * half] = jnp.where(first, imag[:, :1], mirrored(real))
    slab_ref[:, 2 * half : 3 * half] = jnp.where(first, 0.0, imag)
    slab_ref[:, 3 * half :] = jnp.where(first, 0.0, -mirrored(imag))
    weights_ref[...] = jnp.dot(
        total[:, 2 * half :], powers_ref[...], precision=lax.Precision.HIGHEST,
        preferred_element_type=F32,
    )


def finish(received, length, scale):
    rows = received.shape[1]
    return pl.pallas_call(
        finish_kernel,
        out_shape=(
            jax.ShapeDtypeStruct((rows, 2 * length), F32),
            jax.ShapeDtypeStruct((rows, length), F32),
        ),
        name="finish_slab",
    )(received, level_powers(length, scale))


def gather_rows(block, owners, reach, count):
    turn = lambda i: lax.ppermute(block, "owner", [(k, (k + i * count) % owners) for k in range(owners)])
    if reach != 4:
        return [(block,)] + [(turn(i),) for i in range(1, reach)]
    back, ahead = turn(1), turn(3)
    inner = range(count, 3 * count)
    up = lax.ppermute(back, "owner", [(k, k + count) for k in inner])
    down = lax.ppermute(ahead, "owner", [(k, k - count) for k in inner])
    return [(block,), (back,), (up, down), (ahead,)]


def on_device(
    images, defocus, owner_of, pair_of, shift_of, projections, interp_weights, pair_class
):
    particles, lines, length = images.shape
    owners = lax.axis_size("owner")
    capacity = 2 * particles // owners
    pairs, slab_lines, _ = interp_weights.shape
    rows = CLASSES * slab_lines
    reach = max(1, capacity // 4)
    count = owners // reach
    pieces = count if reach > 1 else 1
    moved = sort_particles(
        images, owner_of[:, 0], pair_of, shift_of, defocus, reach, count, reach * capacity, pairs, pieces
    )
    references = gather_rows(fold(projections, interp_weights, pair_class), owners, reach, count)
    if reach > 1:
        swap = lambda a, i: lax.ppermute(a, "owner", [(k, k ^ i) for k in range(owners)]) if i else a
        arrived = [swap(a, i) for i, a in enumerate(moved)]
    else:
        arrived = [lax.all_to_all(moved[0], "owner", split_axis=0, concat_axis=0, tiled=True)]
    partial = score_and_spread(arrived, references, rows, slab_lines, lines, length)
    received = lax.all_to_all(partial, "owner", split_axis=0, concat_axis=0, tiled=True)
    return finish(
        received.reshape(owners, rows // owners, -1), length, CLASSES / (particles * owners)
    )


def solution(mesh):
    return jax.shard_map(
        on_device,
        mesh=mesh,
        in_specs=(
            P(("half", "owner"), None, None),
            P(("half", "owner")),
            P(("half", "owner"), None),
            P(("half", "owner")),
            P(("half", "owner")),
            P(("half", "owner"), None, None),
            P(("half", "owner"), None, None),
            P(("half", "owner")),
        ),
        out_specs=(P(("half", "owner"), None), P(("half", "owner"), None)),
        check_vma=False,
    )
```

```python
import math

import jax
import jax.numpy as jnp
import numpy as np
from jax import lax
from jax.experimental import pallas as pl
from jax.experimental.pallas import tpu as pltpu
from jax.sharding import PartitionSpec as P

CLASSES = 64
LEVELS = 256
F32 = jnp.float32
BF16 = jnp.bfloat16
HBM = pl.BlockSpec(memory_space=pltpu.MemorySpace.HBM)


def vmem(megabytes):
    return pltpu.CompilerParams(vmem_limit_bytes=megabytes * 1024 * 1024)


def packed_table(length):
    half = length // 2
    product = np.arange(length)[:, None] * np.arange(half + 1)[None, :] % length
    angles = product * (2.0 * math.pi / length)
    cosine, sine = np.cos(angles), -np.sin(angles)
    sine[:, 0] = cosine[:, half]
    table = np.concatenate([cosine[:, :half], sine[:, :half]], axis=1) / math.sqrt(length)
    return jnp.asarray(table, F32).astype(BF16)


def mirror(half):
    row = lax.broadcasted_iota(jnp.int32, (half, half), 0)
    column = lax.broadcasted_iota(jnp.int32, (half, half), 1)
    return jnp.where(row + column == half, 1.0, 0.0).astype(BF16)


def put_tiles(ref, values):
    for t in range(ref.shape[0]):
        ref[t] = values[:, t * 128 : (t + 1) * 128]


def every(ref, start, count, stride):
    picked = [ref[t, pl.ds(start, count, stride=stride), :] for t in range(ref.shape[0])]
    return jnp.concatenate(picked, axis=1)


def flipped(rows):
    down, across = rows.shape
    if across < 128:
        rows = jnp.concatenate([rows, jnp.zeros((down, 128 - across), F32)], axis=1)
    if down < 128:
        rows = jnp.concatenate([rows, jnp.zeros((128 - down, 128), F32)], axis=0)
    return rows.T


def short_sine(x):
    square = x * x
    total = jnp.full(x.shape, -1.0 / 39916800.0, F32)
    for factor in (1.0 / 362880.0, -1.0 / 5040.0, 1.0 / 120.0, -1.0 / 6.0, 1.0):
        total = total * square + factor
    return total * x


def sine_of(x):
    turns = jnp.floor(x * (0.5 / math.pi) + 0.5)
    x = ((x - turns * 6.28125) - turns * 0.0019340515136718750) - turns * 1.2556659145e-06
    x = jnp.where(x > 0.5 * math.pi, math.pi - x, jnp.where(x < -0.5 * math.pi, -math.pi - x, x))
    return short_sine(x)


def fold_kernel(x_ref, interp_ref, class_ref, out_ref, folded):
    pairs, width = out_ref.shape
    half = x_ref.shape[1] // 4
    lines = x_ref.shape[0] // pairs
    flip = mirror(half)
    real_low, real_high = x_ref[:, :half], x_ref[:, half : 2 * half]
    imag_low, imag_high = x_ref[:, 2 * half : 3 * half], x_ref[:, 3 * half :]
    real = real_low.astype(F32) + jnp.dot(real_high, flip, preferred_element_type=F32)
    imag = imag_low.astype(F32) - jnp.dot(imag_high, flip, preferred_element_type=F32)
    lane = lax.broadcasted_iota(jnp.int32, imag.shape, 1)
    imag = jnp.where(lane == 0, real_high.astype(F32)[:, :1], imag)
    put_tiles(folded, jnp.concatenate([real, imag], axis=1))
    for line in range(lines):
        out_ref[:, line * 2 * half : (line + 1) * 2 * half] = every(
            folded, line, pairs, lines
        ).astype(BF16)
    label = jnp.broadcast_to(class_ref[...].astype(F32), (8, pairs))
    info = flipped(jnp.concatenate([interp_ref[...].astype(F32), label], axis=0))
    out_ref[:, lines * 2 * half :] = info[:pairs].astype(BF16)


def fold(projections, interp_weights, pair_class):
    pairs, lines, width = projections.shape
    taps = interp_weights.transpose(1, 2, 0).reshape(-1, pairs)
    return pl.pallas_call(
        fold_kernel,
        out_shape=jax.ShapeDtypeStruct((pairs, lines * width // 2 + 128), BF16),
        scratch_shapes=[pltpu.VMEM((width // 256, pairs * lines, 128), F32)],
        compiler_params=vmem(12),
        name="fold_projections",
    )(projections.reshape(pairs * lines, width), taps, pair_class[None, :])


def sort_kernel(reach, count, capacity, pairs, *refs):
    sources, refs = refs[:6], refs[6:]
    *outs, x_ref, owner_ref, pair_ref, shift_ref, defocus_ref, table_ref, wide, sorted_ref, in_sem, x_sem, out_sem = refs
    loads = [
        pltpu.make_async_copy(a, b, in_sem.at[i])
        for i, (a, b) in enumerate(
            zip(sources[1:], (owner_ref, pair_ref, shift_ref, defocus_ref, table_ref))
        )
    ]
    parts = x_sem.shape[0]
    share = x_ref.shape[0] // parts
    cuts = [slice(i * share, (i + 1) * share) for i in range(parts)]
    chunks = [
        pltpu.make_async_copy(sources[0].at[cut], x_ref.at[cut], x_sem.at[i])
        for i, cut in enumerate(cuts)
    ]
    for copy in loads + chunks:
        copy.start()
    particles = owner_ref.shape[1]
    length = x_ref.shape[1]
    half = length // 2
    lines = x_ref.shape[0] // particles
    slots = sorted_ref.shape[0]
    each = slots // len(outs)
    row = lax.broadcasted_iota(jnp.int32, (particles, particles), 0)
    column = lax.broadcasted_iota(jnp.int32, (particles, particles), 1)
    before = jnp.where(row < column, 1.0, 0.0).astype(BF16)
    for load in loads[:4]:
        load.wait()
    me = lax.axis_index("owner")
    owner = owner_ref[...]
    bins = owner & (count - 1)
    if len(outs) > 1:
        bins = bins ^ (me & (count - 1))
    step = ((me >> (count.bit_length() - 1)) - (owner >> (count.bit_length() - 1))) & (reach - 1)
    pair = step * pairs + pair_ref[...]
    padded = -(-count // 8) * 8
    hits = lax.broadcasted_iota(jnp.int32, (padded, particles), 0) == bins
    earlier = jnp.dot(jnp.where(hits, 1.0, 0.0).astype(BF16), before, preferred_element_type=F32)
    earlier = jnp.sum(jnp.where(hits, earlier, 0.0), axis=0, keepdims=True)
    place = bins * capacity + earlier.astype(jnp.int32)
    pick = lax.broadcasted_iota(jnp.int32, (slots, particles), 0) == place
    pick = jnp.where(pick, 1.0, 0.0).astype(BF16)
    defocus = defocus_ref[...].astype(F32)
    level = jnp.where(defocus < 2.0, (defocus - 1.0) * 128.0, 128.0 + (defocus - 2.0) * 64.0)
    kind = lax.broadcasted_iota(jnp.int32, (8, particles), 0)
    facts = jnp.where(kind == 0, jnp.floor(level + 0.5), jnp.ones((8, particles), F32))
    facts = jnp.where(kind == 1, pair.astype(F32), facts)
    facts = jnp.where(kind == 2, shift_ref[...].astype(F32), facts)
    facts = flipped(jnp.where(kind == 4, defocus, facts))
    picked = jnp.dot(pick, facts.astype(BF16), preferred_element_type=F32)
    sorted_ref[:, lines * length :] = picked.astype(BF16)

    column = lax.broadcasted_iota(jnp.int32, (particles, half + 128), 1)
    folded = column.astype(F32) * (1.0 / length)
    ctf = -sine_of(facts[:, 4:5] * 1500.0 * (folded * folded) + 0.2)
    shift = facts[:, 2:3].astype(jnp.int32)
    turn = (shift * column[:, :half]) & (length - 1)
    turn = jnp.where(turn >= half, turn - length, turn).astype(F32) * (2.0 * math.pi / length)
    size = jnp.abs(turn)
    mirrored = jnp.where(size > 0.5 * math.pi, math.pi - size, size)
    swing = short_sine(jnp.where(turn < 0, -mirrored, mirrored))
    cosine = ctf[:, :half] * short_sine(0.5 * math.pi - size)
    nyquist = ctf[:, half : half + 1] * (1 - 2 * (shift & 1)).astype(F32)
    cosine_imag = jnp.where(column[:, :half] == 0, nyquist, cosine)
    sine = ctf[:, :half] * swing

    loads[4].wait()
    for chunk, cut in zip(chunks, cuts):
        chunk.wait()
        spectra = jnp.dot(x_ref[cut], table_ref[...], preferred_element_type=F32)
        spectra = spectra.astype(BF16).astype(F32)
        for t in range(length // 128):
            wide[t, cut] = spectra[:, t * 128 : (t + 1) * 128]
    groups = out_sem.shape[1]
    stores = []
    for line in range(lines):
        spectra = every(wide, line, particles, lines)
        real, imag = spectra[:, :half], spectra[:, half:]
        turned = jnp.concatenate(
            [cosine * real + sine * imag, cosine_imag * imag - sine * real], axis=1
        )
        picked = jnp.dot(pick, turned.astype(BF16), preferred_element_type=F32)
        sorted_ref[:, line * length : (line + 1) * length] = picked.astype(BF16)
        if (line + 1) % (lines // groups) == 0:
            group = line * groups // lines
            wide_group = lines // groups * length
            end = (group + 1) * wide_group + (128 if line == lines - 1 else 0)
            for j, out in enumerate(outs):
                stores.append(
                    pltpu.make_async_copy(
                        sorted_ref.at[j * each : (j + 1) * each, group * wide_group : end],
                        out.at[:, group * wide_group : end],
                        out_sem.at[j, group],
                    )
                )
                stores[-1].start()
    for store in stores:
        store.wait()


def sort_particles(images, owner, pair, shift, defocus, reach, count, capacity, pairs, pieces):
    particles, lines, length = images.shape
    slots = count * capacity
    each, width, groups = slots // pieces, lines * length + 128, 4
    args = [images.reshape(particles * lines, length)] + [a[None, :] for a in (owner, pair, shift, defocus)]
    args.append(packed_table(length))
    return pl.pallas_call(
        lambda *refs: sort_kernel(reach, count, capacity, pairs, *refs),
        in_specs=[HBM] * 6,
        out_specs=[HBM] * pieces,
        out_shape=[jax.ShapeDtypeStruct((each, width), BF16)] * pieces,
        scratch_shapes=[pltpu.VMEM(a.shape, a.dtype) for a in args]
        + [
            pltpu.VMEM((length // 128, particles * lines, 128), F32),
            pltpu.VMEM((slots, width), BF16),
            pltpu.SemaphoreType.DMA((5,)),
            pltpu.SemaphoreType.DMA((2,)),
            pltpu.SemaphoreType.DMA((pieces, groups)),
        ],
        compiler_params=vmem(60),
        name="sort_particles",
    )(*args)


def joined(blocks, at):
    return jnp.concatenate([sum((ref[:, at] for ref in block[1:]), block[0][:, at]) for block in blocks], axis=0)


def score_kernel(scale, n_images, sizes, slab_lines, lines, length, *refs):
    images, refs = refs[:n_images], refs[n_images:]
    blocks = []
    for size in sizes:
        blocks.append(refs[:size])
        refs = refs[size:]
    out_ref, taps = refs
    info = joined(blocks, slice(lines * length, lines * length + 128))
    pairs, rows = info.shape[0], out_ref.shape[0]
    found = jnp.concatenate([ref[:, lines * length :] for ref in images], axis=0).astype(F32)
    slots = found.shape[0]
    here = 4

    def stacked(line):
        return jnp.concatenate(
            [ref[:, line * length : (line + 1) * length] for ref in images], axis=0
        )

    scores = jnp.zeros((slots, pairs), F32)
    for line in range(lines):
        block = joined(blocks, slice(line * length, (line + 1) * length))
        across = block.astype(F32).T.astype(BF16)
        scores = scores + jnp.dot(stacked(line), across, preferred_element_type=F32)

    pair_row = jnp.concatenate(
        [found[t : t + 128].T[1:2] for t in range(0, slots, 128)], axis=1
    ).astype(jnp.int32)
    onehot = lax.broadcasted_iota(jnp.int32, (pairs, slots), 0) == pair_row
    onehot = jnp.where(onehot, 1.0, 0.0).astype(BF16)
    tap = lax.dot_general(info, onehot, (((0,), (0,)), ((), ())), preferred_element_type=F32)
    put_tiles(taps, tap)
    label = tap[slab_lines * lines : slab_lines * lines + 1, :].astype(jnp.int32)
    group = lax.broadcasted_iota(jnp.int32, (rows, slots), 0) // (rows // CLASSES)
    mask = jnp.where(group == label, 1.0, 0.0).astype(BF16).reshape(rows // 16, 16, slots)

    def mixer(tap):
        tap = jnp.concatenate([tap] * (16 // slab_lines), axis=0).astype(BF16)
        return (mask * tap[None]).reshape(rows, slots)

    chosen = lax.broadcasted_iota(jnp.int32, (slots, pairs), 1) == found[:, 1:2].astype(jnp.int32)
    score = jnp.sum(jnp.where(chosen, scores, 0.0), axis=1, keepdims=True)
    weight = found[:, 3:4] / (1.0 + jnp.exp(score * (-2.0 * scale)))
    slab = jnp.zeros((rows, length), F32)
    tap_sum = jnp.zeros((slab_lines, slots), F32)
    for first in range(0, lines, here):
        mixers, contribs = [], []
        for line in range(first, first + here):
            tap = every(taps, line, slab_lines, lines)
            tap_sum = tap_sum + tap
            mixers.append(mixer(tap))
            contribs.append((weight * stacked(line).astype(F32)).astype(BF16))
        slab = slab + jnp.dot(
            jnp.concatenate(mixers, axis=1), jnp.concatenate(contribs, axis=0),
            preferred_element_type=F32,
        )
    out_ref[:, :length] = slab.astype(BF16)
    levels = lax.broadcasted_iota(jnp.int32, (slots, LEVELS), 1) == found[:, :1].astype(jnp.int32)
    levels = jnp.where(levels, weight, 0.0).astype(BF16)
    levels = jnp.dot(mixer(tap_sum), levels, preferred_element_type=F32)
    out_ref[:, length:] = levels.astype(BF16)


def score_and_spread(images, references, rows, slab_lines, lines, length):
    slots = sum(a.shape[0] for a in images)
    sizes = [len(a) for a in references]
    references = [a for blocks in references for a in blocks]
    return pl.pallas_call(
        lambda *refs: score_kernel(
            1.0 / math.sqrt(lines * length), len(images), sizes, slab_lines, lines, length, *refs
        ),
        out_shape=jax.ShapeDtypeStruct((rows, length + LEVELS), BF16),
        scratch_shapes=[pltpu.VMEM((slots // 128, 128, 128), F32)],
        compiler_params=vmem(24),
        name="score_and_spread",
    )(*images, *references)


def level_powers(length, scale):
    level = np.arange(LEVELS)
    defocus = np.where(level < 128, 1.0 + level / 128.0, 2.0 + (level - 128) / 64.0).astype(np.float32)
    column = np.arange(length)
    folded = np.minimum(column, length - column).astype(np.float32) / np.float32(length)
    phase = (defocus * np.float32(1500.0))[:, None] * (folded * folded)[None, :] + np.float32(0.2)
    powers = np.sin(phase.astype(np.float64)) ** 2 * scale
    powers = np.where(level[:, None] <= 192, powers, 0.0)
    coarse = powers.astype(jnp.bfloat16)
    fine = (powers - coarse.astype(np.float64)).astype(jnp.bfloat16)
    return jnp.asarray(np.stack([coarse, fine]))


def pieces_of(values, count):
    pieces = []
    for _ in range(count):
        pieces.append(values.astype(BF16))
        values = values - pieces[-1].astype(F32)
    return jnp.concatenate([piece.astype(F32) for piece in pieces], axis=0).astype(BF16)


def finish_kernel(x_ref, powers_ref, slab_ref, weights_ref):
    rows, half = slab_ref.shape[0], slab_ref.shape[1] // 4
    total = jnp.sum(x_ref[...].astype(F32), axis=0)
    real, imag = total[:, :half], total[:, half : 2 * half]
    both = pieces_of(jnp.concatenate([real, imag], axis=0), 3)
    turned = jnp.dot(both, mirror(half), preferred_element_type=F32)
    turned = turned[: 2 * rows] + turned[2 * rows : 4 * rows] + turned[4 * rows :]
    first = lax.broadcasted_iota(jnp.int32, real.shape, 1) == 0
    slab_ref[:, :half] = real
    slab_ref[:, half : 2 * half] = jnp.where(first, imag[:, :1], turned[:rows])
    slab_ref[:, 2 * half : 3 * half] = jnp.where(first, 0.0, imag)
    slab_ref[:, 3 * half :] = jnp.where(first, 0.0, -turned[rows:])
    levels = pieces_of(total[:, 2 * half :], 2)
    coarse = jnp.dot(levels, powers_ref[0], preferred_element_type=F32)
    fine = jnp.dot(levels[:rows], powers_ref[1], preferred_element_type=F32)
    weights_ref[...] = coarse[:rows] + coarse[rows:] + fine


def finish(received, length, scale):
    rows = received.shape[1]
    return pl.pallas_call(
        finish_kernel,
        out_shape=(
            jax.ShapeDtypeStruct((rows, 2 * length), F32),
            jax.ShapeDtypeStruct((rows, length), F32),
        ),
        name="finish_slab",
    )(received, level_powers(length, scale))


def gather_rows(block, owners, reach, count):
    turn = lambda i: lax.ppermute(block, "owner", [(k, (k + i * count) % owners) for k in range(owners)])
    if reach != 4:
        return [(block,)] + [(turn(i),) for i in range(1, reach)]
    back, ahead = turn(1), turn(3)
    inner = range(count, 3 * count)
    up = lax.ppermute(back, "owner", [(k, k + count) for k in inner])
    down = lax.ppermute(ahead, "owner", [(k, k - count) for k in inner])
    return [(block,), (back,), (up, down), (ahead,)]


def on_device(
    images, defocus, owner_of, pair_of, shift_of, projections, interp_weights, pair_class
):
    particles, lines, length = images.shape
    owners = lax.axis_size("owner")
    capacity = 2 * particles // owners
    pairs, slab_lines, _ = interp_weights.shape
    rows = CLASSES * slab_lines
    reach = max(1, capacity // 4)
    count = owners // reach
    pieces = count if reach > 1 else 1
    moved = sort_particles(
        images, owner_of[:, 0], pair_of, shift_of, defocus, reach, count, reach * capacity, pairs, pieces
    )
    references = gather_rows(fold(projections, interp_weights, pair_class), owners, reach, count)
    if reach > 1:
        swap = lambda a, i: lax.ppermute(a, "owner", [(k, k ^ i) for k in range(owners)]) if i else a
        arrived = [swap(a, i) for i, a in enumerate(moved)]
    else:
        arrived = [lax.all_to_all(moved[0], "owner", split_axis=0, concat_axis=0, tiled=True)]
    partial = score_and_spread(arrived, references, rows, slab_lines, lines, length)
    received = lax.all_to_all(partial, "owner", split_axis=0, concat_axis=0, tiled=True)
    return finish(
        received.reshape(owners, rows // owners, -1), length, CLASSES / (particles * owners)
    )


def solution(mesh):
    return jax.shard_map(
        on_device,
        mesh=mesh,
        in_specs=(
            P(("half", "owner"), None, None),
            P(("half", "owner")),
            P(("half", "owner"), None),
            P(("half", "owner")),
            P(("half", "owner")),
            P(("half", "owner"), None, None),
            P(("half", "owner"), None, None),
            P(("half", "owner")),
        ),
        out_specs=(P(("half", "owner"), None), P(("half", "owner"), None)),
        check_vma=False,
    )
```

```python
import math

import jax
import jax.numpy as jnp
import numpy as np
from jax import lax
from jax.experimental import pallas as pl
from jax.experimental.pallas import tpu as pltpu
from jax.sharding import PartitionSpec as P

CLASSES = 64
LEVELS = 256
F32 = jnp.float32
BF16 = jnp.bfloat16
HBM = pl.BlockSpec(memory_space=pltpu.MemorySpace.HBM)


def vmem(megabytes):
    return pltpu.CompilerParams(vmem_limit_bytes=megabytes * 1024 * 1024)


def packed_table(length):
    half = length // 2
    product = np.arange(length)[:, None] * np.arange(half + 1)[None, :] % length
    angles = product * (2.0 * math.pi / length)
    cosine, sine = np.cos(angles), -np.sin(angles)
    sine[:, 0] = cosine[:, half]
    table = np.concatenate([cosine[:, :half], sine[:, :half]], axis=1) / math.sqrt(length)
    return jnp.asarray(table, F32).astype(BF16)


def mirror(half):
    row = lax.broadcasted_iota(jnp.int32, (half, half), 0)
    column = lax.broadcasted_iota(jnp.int32, (half, half), 1)
    return jnp.where(row + column == half, 1.0, 0.0).astype(BF16)


def put_tiles(ref, values):
    for t in range(ref.shape[0]):
        ref[t] = values[:, t * 128 : (t + 1) * 128]


def every(ref, start, count, stride):
    picked = [ref[t, pl.ds(start, count, stride=stride), :] for t in range(ref.shape[0])]
    return jnp.concatenate(picked, axis=1)


def flipped(rows):
    down, across = rows.shape
    if across < 128:
        rows = jnp.concatenate([rows, jnp.zeros((down, 128 - across), F32)], axis=1)
    if down < 128:
        rows = jnp.concatenate([rows, jnp.zeros((128 - down, 128), F32)], axis=0)
    return rows.T


def short_sine(x):
    square = x * x
    total = jnp.full(x.shape, -1.0 / 39916800.0, F32)
    for factor in (1.0 / 362880.0, -1.0 / 5040.0, 1.0 / 120.0, -1.0 / 6.0, 1.0):
        total = total * square + factor
    return total * x


def sine_of(x):
    turns = jnp.floor(x * (0.5 / math.pi) + 0.5)
    x = ((x - turns * 6.28125) - turns * 0.0019340515136718750) - turns * 1.2556659145e-06
    x = jnp.where(x > 0.5 * math.pi, math.pi - x, jnp.where(x < -0.5 * math.pi, -math.pi - x, x))
    return short_sine(x)


def fold_kernel(x_ref, interp_ref, class_ref, out_ref, folded):
    pairs, width = out_ref.shape
    half = x_ref.shape[1] // 4
    lines = x_ref.shape[0] // pairs
    flip = mirror(half)
    real_low, real_high = x_ref[:, :half], x_ref[:, half : 2 * half]
    imag_low, imag_high = x_ref[:, 2 * half : 3 * half], x_ref[:, 3 * half :]
    real = real_low.astype(F32) + jnp.dot(real_high, flip, preferred_element_type=F32)
    imag = imag_low.astype(F32) - jnp.dot(imag_high, flip, preferred_element_type=F32)
    lane = lax.broadcasted_iota(jnp.int32, imag.shape, 1)
    imag = jnp.where(lane == 0, real_high.astype(F32)[:, :1], imag)
    put_tiles(folded, jnp.concatenate([real, imag], axis=1))
    for line in range(lines):
        out_ref[:, line * 2 * half : (line + 1) * 2 * half] = every(
            folded, line, pairs, lines
        ).astype(BF16)
    label = jnp.broadcast_to(class_ref[...].astype(F32), (8, pairs))
    info = flipped(jnp.concatenate([interp_ref[...].astype(F32), label], axis=0))
    out_ref[:, lines * 2 * half :] = info[:pairs].astype(BF16)


def fold(projections, interp_weights, pair_class):
    pairs, lines, width = projections.shape
    taps = interp_weights.transpose(1, 2, 0).reshape(-1, pairs)
    return pl.pallas_call(
        fold_kernel,
        out_shape=jax.ShapeDtypeStruct((pairs, lines * width // 2 + 128), BF16),
        scratch_shapes=[pltpu.VMEM((width // 256, pairs * lines, 128), F32)],
        compiler_params=vmem(12),
        name="fold_projections",
    )(projections.reshape(pairs * lines, width), taps, pair_class[None, :])


def sort_kernel(first, reach, count, capacity, pairs, *refs):
    sources, refs = refs[:6], refs[6:]
    *outs, x_ref, owner_ref, pair_ref, shift_ref, defocus_ref, table_ref, wide, sorted_ref, in_sem, x_sem, out_sem = refs
    loads = [
        pltpu.make_async_copy(a, b, in_sem.at[i])
        for i, (a, b) in enumerate(
            zip(sources[1:], (owner_ref, pair_ref, shift_ref, defocus_ref, table_ref))
        )
    ]
    parts = x_sem.shape[0]
    particles, lines, length = x_ref.shape
    share = particles // parts
    cuts = [slice(i * share, (i + 1) * share) for i in range(parts)]
    chunks = [
        pltpu.make_async_copy(sources[0].at[cut, first : first + lines], x_ref.at[cut], x_sem.at[i])
        for i, cut in enumerate(cuts)
    ]
    for copy in loads + chunks:
        copy.start()
    half = length // 2
    slots = sorted_ref.shape[0]
    each = slots // len(outs)
    row = lax.broadcasted_iota(jnp.int32, (particles, particles), 0)
    column = lax.broadcasted_iota(jnp.int32, (particles, particles), 1)
    before = jnp.where(row < column, 1.0, 0.0).astype(BF16)
    for load in loads[:4]:
        load.wait()
    me = lax.axis_index("owner")
    owner = owner_ref[...]
    bins = owner & (count - 1)
    if len(outs) > 1:
        bins = bins ^ (me & (count - 1))
    step = ((me >> (count.bit_length() - 1)) - (owner >> (count.bit_length() - 1))) & (reach - 1)
    pair = step * pairs + pair_ref[...]
    padded = -(-count // 8) * 8
    hits = lax.broadcasted_iota(jnp.int32, (padded, particles), 0) == bins
    earlier = jnp.dot(jnp.where(hits, 1.0, 0.0).astype(BF16), before, preferred_element_type=F32)
    earlier = jnp.sum(jnp.where(hits, earlier, 0.0), axis=0, keepdims=True)
    place = bins * capacity + earlier.astype(jnp.int32)
    pick = lax.broadcasted_iota(jnp.int32, (slots, particles), 0) == place
    pick = jnp.where(pick, 1.0, 0.0).astype(BF16)
    defocus = defocus_ref[...].astype(F32)
    level = jnp.where(defocus < 2.0, (defocus - 1.0) * 128.0, 128.0 + (defocus - 2.0) * 64.0)
    kind = lax.broadcasted_iota(jnp.int32, (8, particles), 0)
    facts = jnp.where(kind == 0, jnp.floor(level + 0.5), jnp.ones((8, particles), F32))
    facts = jnp.where(kind == 1, pair.astype(F32), facts)
    facts = jnp.where(kind == 2, shift_ref[...].astype(F32), facts)
    facts = flipped(jnp.where(kind == 4, defocus, facts))
    extra = 0 if first else 128
    if extra:
        picked = jnp.dot(pick, facts.astype(BF16), preferred_element_type=F32)
        sorted_ref[:, lines * length :] = picked.astype(BF16)

    column = lax.broadcasted_iota(jnp.int32, (particles, half + 128), 1)
    folded = column.astype(F32) * (1.0 / length)
    ctf = -sine_of(facts[:, 4:5] * 1500.0 * (folded * folded) + 0.2)
    shift = facts[:, 2:3].astype(jnp.int32)
    turn = (shift * column[:, :half]) & (length - 1)
    turn = jnp.where(turn >= half, turn - length, turn).astype(F32) * (2.0 * math.pi / length)
    size = jnp.abs(turn)
    mirrored = jnp.where(size > 0.5 * math.pi, math.pi - size, size)
    swing = short_sine(jnp.where(turn < 0, -mirrored, mirrored))
    cosine = ctf[:, :half] * short_sine(0.5 * math.pi - size)
    nyquist = ctf[:, half : half + 1] * (1 - 2 * (shift & 1)).astype(F32)
    cosine_imag = jnp.where(column[:, :half] == 0, nyquist, cosine)
    sine = ctf[:, :half] * swing

    loads[4].wait()
    for i, (chunk, cut) in enumerate(zip(chunks, cuts)):
        chunk.wait()
        rows = x_ref[cut].reshape(share * lines, length)
        spectra = jnp.dot(rows, table_ref[...], preferred_element_type=F32)
        spectra = spectra.astype(BF16).astype(F32)
        for t in range(length // 128):
            wide[t, i * share * lines : (i + 1) * share * lines] = spectra[:, t * 128 : (t + 1) * 128]
    groups = out_sem.shape[1]
    stores = []
    for line in range(lines):
        spectra = every(wide, line, particles, lines)
        real, imag = spectra[:, :half], spectra[:, half:]
        turned = jnp.concatenate(
            [cosine * real + sine * imag, cosine_imag * imag - sine * real], axis=1
        )
        picked = jnp.dot(pick, turned.astype(BF16), preferred_element_type=F32)
        sorted_ref[:, line * length : (line + 1) * length] = picked.astype(BF16)
        if (line + 1) % (lines // groups) == 0:
            group = line * groups // lines
            wide_group = lines // groups * length
            end = (group + 1) * wide_group + (extra if line == lines - 1 else 0)
            for j, out in enumerate(outs):
                stores.append(
                    pltpu.make_async_copy(
                        sorted_ref.at[j * each : (j + 1) * each, group * wide_group : end],
                        out.at[:, group * wide_group : end],
                        out_sem.at[j, group],
                    )
                )
                stores[-1].start()
    for store in stores:
        store.wait()


def sort_particles(first, lines, images, owner, pair, shift, defocus, reach, count, capacity, pairs, pieces):
    particles, _, length = images.shape
    slots = count * capacity
    each, width, groups = slots // pieces, lines * length + (0 if first else 128), 4
    args = [images] + [a[None, :] for a in (owner, pair, shift, defocus)]
    args.append(packed_table(length))
    return pl.pallas_call(
        lambda *refs: sort_kernel(first, reach, count, capacity, pairs, *refs),
        in_specs=[HBM] * 6,
        out_specs=[HBM] * pieces,
        out_shape=[jax.ShapeDtypeStruct((each, width), BF16)] * pieces,
        scratch_shapes=[pltpu.VMEM((particles, lines, length), BF16)]
        + [pltpu.VMEM(a.shape, a.dtype) for a in args[1:]]
        + [
            pltpu.VMEM((length // 128, particles * lines, 128), F32),
            pltpu.VMEM((slots, width), BF16),
            pltpu.SemaphoreType.DMA((5,)),
            pltpu.SemaphoreType.DMA((2,)),
            pltpu.SemaphoreType.DMA((pieces, groups)),
        ],
        compiler_params=vmem(60),
        name="sort_particles",
    )(*args)


def joined(blocks, at):
    return jnp.concatenate([sum((ref[:, at] for ref in block[1:]), block[0][:, at]) for block in blocks], axis=0)


def score_kernel(scale, n_images, sizes, slab_lines, lines, length, *refs):
    images, refs = refs[:n_images], refs[n_images:]
    later, refs = refs[:n_images], refs[n_images:]
    early = images[0].shape[1] // length
    blocks = []
    for size in sizes:
        blocks.append(refs[:size])
        refs = refs[size:]
    out_ref, taps = refs
    info = joined(blocks, slice(lines * length, lines * length + 128))
    pairs, rows = info.shape[0], out_ref.shape[0]
    found = jnp.concatenate([ref[:, early * length :] for ref in images], axis=0).astype(F32)
    slots = found.shape[0]
    here = 4

    def stacked(line):
        refs, place = (images, line) if line < early else (later, line - early)
        return jnp.concatenate(
            [ref[:, place * length : (place + 1) * length] for ref in refs], axis=0
        )

    scores = jnp.zeros((slots, pairs), F32)
    for line in range(lines):
        block = joined(blocks, slice(line * length, (line + 1) * length))
        across = block.astype(F32).T.astype(BF16)
        scores = scores + jnp.dot(stacked(line), across, preferred_element_type=F32)

    pair_row = jnp.concatenate(
        [found[t : t + 128].T[1:2] for t in range(0, slots, 128)], axis=1
    ).astype(jnp.int32)
    onehot = lax.broadcasted_iota(jnp.int32, (pairs, slots), 0) == pair_row
    onehot = jnp.where(onehot, 1.0, 0.0).astype(BF16)
    tap = lax.dot_general(info, onehot, (((0,), (0,)), ((), ())), preferred_element_type=F32)
    put_tiles(taps, tap)
    label = tap[slab_lines * lines : slab_lines * lines + 1, :].astype(jnp.int32)
    group = lax.broadcasted_iota(jnp.int32, (rows, slots), 0) // (rows // CLASSES)
    mask = jnp.where(group == label, 1.0, 0.0).astype(BF16).reshape(rows // 16, 16, slots)

    def mixer(tap):
        tap = jnp.concatenate([tap] * (16 // slab_lines), axis=0).astype(BF16)
        return (mask * tap[None]).reshape(rows, slots)

    chosen = lax.broadcasted_iota(jnp.int32, (slots, pairs), 1) == found[:, 1:2].astype(jnp.int32)
    score = jnp.sum(jnp.where(chosen, scores, 0.0), axis=1, keepdims=True)
    weight = found[:, 3:4] / (1.0 + jnp.exp(score * (-2.0 * scale)))
    slab = jnp.zeros((rows, length), F32)
    tap_sum = jnp.zeros((slab_lines, slots), F32)
    for first in range(0, lines, here):
        mixers, contribs = [], []
        for line in range(first, first + here):
            tap = every(taps, line, slab_lines, lines)
            tap_sum = tap_sum + tap
            mixers.append(mixer(tap))
            contribs.append((weight * stacked(line).astype(F32)).astype(BF16))
        slab = slab + jnp.dot(
            jnp.concatenate(mixers, axis=1), jnp.concatenate(contribs, axis=0),
            preferred_element_type=F32,
        )
    out_ref[:, :length] = slab.astype(BF16)
    levels = lax.broadcasted_iota(jnp.int32, (slots, LEVELS), 1) == found[:, :1].astype(jnp.int32)
    levels = jnp.where(levels, weight, 0.0).astype(BF16)
    levels = jnp.dot(mixer(tap_sum), levels, preferred_element_type=F32)
    out_ref[:, length:] = levels.astype(BF16)


def score_and_spread(images, later, references, rows, slab_lines, lines, length):
    slots = sum(a.shape[0] for a in images)
    sizes = [len(a) for a in references]
    references = [a for blocks in references for a in blocks]
    return pl.pallas_call(
        lambda *refs: score_kernel(
            1.0 / math.sqrt(lines * length), len(images), sizes, slab_lines, lines, length, *refs
        ),
        out_shape=jax.ShapeDtypeStruct((rows, length + LEVELS), BF16),
        scratch_shapes=[pltpu.VMEM((slots // 128, 128, 128), F32)],
        compiler_params=vmem(24),
        name="score_and_spread",
    )(*images, *later, *references)


def level_powers(length, scale):
    level = np.arange(LEVELS)
    defocus = np.where(level < 128, 1.0 + level / 128.0, 2.0 + (level - 128) / 64.0).astype(np.float32)
    column = np.arange(length)
    folded = np.minimum(column, length - column).astype(np.float32) / np.float32(length)
    phase = (defocus * np.float32(1500.0))[:, None] * (folded * folded)[None, :] + np.float32(0.2)
    powers = np.sin(phase.astype(np.float64)) ** 2 * scale
    powers = np.where(level[:, None] <= 192, powers, 0.0)
    coarse = powers.astype(jnp.bfloat16)
    fine = (powers - coarse.astype(np.float64)).astype(jnp.bfloat16)
    return jnp.asarray(np.stack([coarse, fine]))


def pieces_of(values, count):
    pieces = []
    for _ in range(count):
        pieces.append(values.astype(BF16))
        values = values - pieces[-1].astype(F32)
    return jnp.concatenate([piece.astype(F32) for piece in pieces], axis=0).astype(BF16)


def finish_kernel(x_ref, powers_ref, slab_ref, weights_ref):
    rows, half = slab_ref.shape[0], slab_ref.shape[1] // 4
    total = jnp.sum(x_ref[...].astype(F32), axis=0)
    real, imag = total[:, :half], total[:, half : 2 * half]
    both = pieces_of(jnp.concatenate([real, imag], axis=0), 3)
    turned = jnp.dot(both, mirror(half), preferred_element_type=F32)
    turned = turned[: 2 * rows] + turned[2 * rows : 4 * rows] + turned[4 * rows :]
    first = lax.broadcasted_iota(jnp.int32, real.shape, 1) == 0
    slab_ref[:, :half] = real
    slab_ref[:, half : 2 * half] = jnp.where(first, imag[:, :1], turned[:rows])
    slab_ref[:, 2 * half : 3 * half] = jnp.where(first, 0.0, imag)
    slab_ref[:, 3 * half :] = jnp.where(first, 0.0, -turned[rows:])
    levels = pieces_of(total[:, 2 * half :], 2)
    coarse = jnp.dot(levels, powers_ref[0], preferred_element_type=F32)
    fine = jnp.dot(levels[:rows], powers_ref[1], preferred_element_type=F32)
    weights_ref[...] = coarse[:rows] + coarse[rows:] + fine


def finish(received, length, scale):
    rows = received.shape[1]
    return pl.pallas_call(
        finish_kernel,
        out_shape=(
            jax.ShapeDtypeStruct((rows, 2 * length), F32),
            jax.ShapeDtypeStruct((rows, length), F32),
        ),
        name="finish_slab",
    )(received, level_powers(length, scale))


def gather_rows(block, owners, reach, count):
    turn = lambda i: lax.ppermute(block, "owner", [(k, (k + i * count) % owners) for k in range(owners)])
    if reach != 4:
        return [(block,)] + [(turn(i),) for i in range(1, reach)]
    back, ahead = turn(1), turn(3)
    inner = range(count, 3 * count)
    up = lax.ppermute(back, "owner", [(k, k + count) for k in inner])
    down = lax.ppermute(ahead, "owner", [(k, k - count) for k in inner])
    return [(block,), (back,), (up, down), (ahead,)]


def on_device(
    images, defocus, owner_of, pair_of, shift_of, projections, interp_weights, pair_class
):
    particles, lines, length = images.shape
    owners = lax.axis_size("owner")
    capacity = 2 * particles // owners
    pairs, slab_lines, _ = interp_weights.shape
    rows = CLASSES * slab_lines
    reach = max(1, capacity // 4)
    count = owners // reach
    pieces = count if reach > 1 else 1
    early = lines // 2
    swap = lambda a, i: lax.ppermute(a, "owner", [(k, k ^ i) for k in range(owners)]) if i else a
    arrived = []
    for first, some in ((0, early), (early, lines - early)):
        moved = sort_particles(
            first, some, images, owner_of[:, 0], pair_of, shift_of, defocus, reach, count,
            reach * capacity, pairs, pieces,
        )
        if reach > 1:
            arrived.append([swap(a, i) for i, a in enumerate(moved)])
        else:
            send = lambda a: lax.all_to_all(a, "owner", split_axis=0, concat_axis=0, tiled=True)
            arrived.append([send(moved[0])])
    references = gather_rows(fold(projections, interp_weights, pair_class), owners, reach, count)
    partial = score_and_spread(*arrived, references, rows, slab_lines, lines, length)
    received = lax.all_to_all(partial, "owner", split_axis=0, concat_axis=0, tiled=True)
    return finish(
        received.reshape(owners, rows // owners, -1), length, CLASSES / (particles * owners)
    )


def solution(mesh):
    return jax.shard_map(
        on_device,
        mesh=mesh,
        in_specs=(
            P(("half", "owner"), None, None),
            P(("half", "owner")),
            P(("half", "owner"), None),
            P(("half", "owner")),
            P(("half", "owner")),
            P(("half", "owner"), None, None),
            P(("half", "owner"), None, None),
            P(("half", "owner")),
        ),
        out_specs=(P(("half", "owner"), None), P(("half", "owner"), None)),
        check_vma=False,
    )
```

```python
import math

import jax
import jax.numpy as jnp
import numpy as np
from jax import lax
from jax.experimental import pallas as pl
from jax.experimental.pallas import tpu as pltpu
from jax.sharding import PartitionSpec as P

CLASSES = 64
LEVELS = 256
F32 = jnp.float32
BF16 = jnp.bfloat16
HBM = pl.BlockSpec(memory_space=pltpu.MemorySpace.HBM)


def vmem(megabytes):
    return pltpu.CompilerParams(vmem_limit_bytes=megabytes * 1024 * 1024)


def packed_table(length):
    half = length // 2
    product = np.arange(length)[:, None] * np.arange(half + 1)[None, :] % length
    angles = product * (2.0 * math.pi / length)
    cosine, sine = np.cos(angles), -np.sin(angles)
    sine[:, 0] = cosine[:, half]
    table = np.concatenate([cosine[:, :half], sine[:, :half]], axis=1) / math.sqrt(length)
    return jnp.asarray(table, F32).astype(BF16)


def mirror(half):
    row = lax.broadcasted_iota(jnp.int32, (half, half), 0)
    column = lax.broadcasted_iota(jnp.int32, (half, half), 1)
    return jnp.where(row + column == half, 1.0, 0.0).astype(BF16)


def put_tiles(ref, values):
    for t in range(ref.shape[0]):
        ref[t] = values[:, t * 128 : (t + 1) * 128]


def every(ref, start, count, stride):
    picked = [ref[t, pl.ds(start, count, stride=stride), :] for t in range(ref.shape[0])]
    return jnp.concatenate(picked, axis=1)


def flipped(rows):
    down, across = rows.shape
    if across < 128:
        rows = jnp.concatenate([rows, jnp.zeros((down, 128 - across), F32)], axis=1)
    if down < 128:
        rows = jnp.concatenate([rows, jnp.zeros((128 - down, 128), F32)], axis=0)
    return rows.T


def short_sine(x):
    square = x * x
    total = jnp.full(x.shape, -1.0 / 39916800.0, F32)
    for factor in (1.0 / 362880.0, -1.0 / 5040.0, 1.0 / 120.0, -1.0 / 6.0, 1.0):
        total = total * square + factor
    return total * x


def sine_of(x):
    turns = jnp.floor(x * (0.5 / math.pi) + 0.5)
    x = ((x - turns * 6.28125) - turns * 0.0019340515136718750) - turns * 1.2556659145e-06
    x = jnp.where(x > 0.5 * math.pi, math.pi - x, jnp.where(x < -0.5 * math.pi, -math.pi - x, x))
    return short_sine(x)


def fold_kernel(x_ref, interp_ref, class_ref, out_ref, folded):
    pairs, width = out_ref.shape
    half = x_ref.shape[1] // 4
    lines = x_ref.shape[0] // pairs
    flip = mirror(half)
    real_low, real_high = x_ref[:, :half], x_ref[:, half : 2 * half]
    imag_low, imag_high = x_ref[:, 2 * half : 3 * half], x_ref[:, 3 * half :]
    real = real_low.astype(F32) + jnp.dot(real_high, flip, preferred_element_type=F32)
    imag = imag_low.astype(F32) - jnp.dot(imag_high, flip, preferred_element_type=F32)
    lane = lax.broadcasted_iota(jnp.int32, imag.shape, 1)
    imag = jnp.where(lane == 0, real_high.astype(F32)[:, :1], imag)
    put_tiles(folded, jnp.concatenate([real, imag], axis=1))
    for line in range(lines):
        out_ref[:, line * 2 * half : (line + 1) * 2 * half] = every(
            folded, line, pairs, lines
        ).astype(BF16)
    label = jnp.broadcast_to(class_ref[...].astype(F32), (8, pairs))
    info = flipped(jnp.concatenate([interp_ref[...].astype(F32), label], axis=0))
    out_ref[:, lines * 2 * half :] = info[:pairs].astype(BF16)


def fold(projections, interp_weights, pair_class):
    pairs, lines, width = projections.shape
    taps = interp_weights.transpose(1, 2, 0).reshape(-1, pairs)
    return pl.pallas_call(
        fold_kernel,
        out_shape=jax.ShapeDtypeStruct((pairs, lines * width // 2 + 128), BF16),
        scratch_shapes=[pltpu.VMEM((width // 256, pairs * lines, 128), F32)],
        compiler_params=vmem(12),
        name="fold_projections",
    )(projections.reshape(pairs * lines, width), taps, pair_class[None, :])


def sort_kernel(first, reach, count, capacity, pairs, *refs):
    sources, refs = refs[:6], refs[6:]
    *outs, x_ref, owner_ref, pair_ref, shift_ref, defocus_ref, table_ref, wide, sorted_ref, in_sem, x_sem, out_sem = refs
    loads = [
        pltpu.make_async_copy(a, b, in_sem.at[i])
        for i, (a, b) in enumerate(
            zip(sources[1:], (owner_ref, pair_ref, shift_ref, defocus_ref, table_ref))
        )
    ]
    parts = x_sem.shape[0]
    particles, lines, length = x_ref.shape
    share = particles // parts
    cuts = [slice(i * share, (i + 1) * share) for i in range(parts)]
    chunks = [
        pltpu.make_async_copy(sources[0].at[cut, first : first + lines], x_ref.at[cut], x_sem.at[i])
        for i, cut in enumerate(cuts)
    ]
    for copy in loads + chunks:
        copy.start()
    half = length // 2
    slots = sorted_ref.shape[0]
    each = slots // len(outs)
    row = lax.broadcasted_iota(jnp.int32, (particles, particles), 0)
    column = lax.broadcasted_iota(jnp.int32, (particles, particles), 1)
    before = jnp.where(row < column, 1.0, 0.0).astype(BF16)
    for load in loads[:4]:
        load.wait()
    me = lax.axis_index("owner")
    owner = owner_ref[...]
    bins = owner & (count - 1)
    if len(outs) > 1:
        bins = bins ^ (me & (count - 1))
    step = ((me >> (count.bit_length() - 1)) - (owner >> (count.bit_length() - 1))) & (reach - 1)
    pair = step * pairs + pair_ref[...]
    padded = -(-count // 8) * 8
    hits = lax.broadcasted_iota(jnp.int32, (padded, particles), 0) == bins
    earlier = jnp.dot(jnp.where(hits, 1.0, 0.0).astype(BF16), before, preferred_element_type=F32)
    earlier = jnp.sum(jnp.where(hits, earlier, 0.0), axis=0, keepdims=True)
    place = bins * capacity + earlier.astype(jnp.int32)
    pick = lax.broadcasted_iota(jnp.int32, (slots, particles), 0) == place
    pick = jnp.where(pick, 1.0, 0.0).astype(BF16)
    defocus = defocus_ref[...].astype(F32)
    level = jnp.where(defocus < 2.0, (defocus - 1.0) * 128.0, 128.0 + (defocus - 2.0) * 64.0)
    kind = lax.broadcasted_iota(jnp.int32, (8, particles), 0)
    facts = jnp.where(kind == 0, jnp.floor(level + 0.5), jnp.ones((8, particles), F32))
    facts = jnp.where(kind == 1, pair.astype(F32), facts)
    facts = jnp.where(kind == 2, shift_ref[...].astype(F32), facts)
    facts = flipped(jnp.where(kind == 4, defocus, facts))
    extra = 0 if first else 128
    if extra:
        picked = jnp.dot(pick, facts.astype(BF16), preferred_element_type=F32)
        sorted_ref[:, lines * length :] = picked.astype(BF16)

    column = lax.broadcasted_iota(jnp.int32, (particles, half + 128), 1)
    folded = column.astype(F32) * (1.0 / length)
    ctf = -sine_of(facts[:, 4:5] * 1500.0 * (folded * folded) + 0.2)
    shift = facts[:, 2:3].astype(jnp.int32)
    turn = (shift * column[:, :half]) & (length - 1)
    turn = jnp.where(turn >= half, turn - length, turn).astype(F32) * (2.0 * math.pi / length)
    size = jnp.abs(turn)
    mirrored = jnp.where(size > 0.5 * math.pi, math.pi - size, size)
    swing = short_sine(jnp.where(turn < 0, -mirrored, mirrored))
    cosine = ctf[:, :half] * short_sine(0.5 * math.pi - size)
    nyquist = ctf[:, half : half + 1] * (1 - 2 * (shift & 1)).astype(F32)
    cosine_imag = jnp.where(column[:, :half] == 0, nyquist, cosine)
    sine = ctf[:, :half] * swing

    loads[4].wait()
    for i, (chunk, cut) in enumerate(zip(chunks, cuts)):
        chunk.wait()
        rows = x_ref[cut].reshape(share * lines, length)
        spectra = jnp.dot(rows, table_ref[...], preferred_element_type=F32)
        spectra = spectra.astype(BF16).astype(F32)
        for t in range(length // 128):
            wide[t, i * share * lines : (i + 1) * share * lines] = spectra[:, t * 128 : (t + 1) * 128]
    groups = out_sem.shape[1]
    stores = []
    for line in range(lines):
        spectra = every(wide, line, particles, lines)
        real, imag = spectra[:, :half], spectra[:, half:]
        turned = jnp.concatenate(
            [cosine * real + sine * imag, cosine_imag * imag - sine * real], axis=1
        )
        picked = jnp.dot(pick, turned.astype(BF16), preferred_element_type=F32)
        sorted_ref[:, line * length : (line + 1) * length] = picked.astype(BF16)
        if (line + 1) % (lines // groups) == 0:
            group = line * groups // lines
            wide_group = lines // groups * length
            end = (group + 1) * wide_group + (extra if line == lines - 1 else 0)
            for j, out in enumerate(outs):
                stores.append(
                    pltpu.make_async_copy(
                        sorted_ref.at[j * each : (j + 1) * each, group * wide_group : end],
                        out.at[:, group * wide_group : end],
                        out_sem.at[j, group],
                    )
                )
                stores[-1].start()
    for store in stores:
        store.wait()


def sort_particles(first, lines, images, owner, pair, shift, defocus, reach, count, capacity, pairs, pieces):
    particles, _, length = images.shape
    slots = count * capacity
    each, width, groups = slots // pieces, lines * length + (0 if first else 128), 2
    args = [images] + [a[None, :] for a in (owner, pair, shift, defocus)]
    args.append(packed_table(length))
    return pl.pallas_call(
        lambda *refs: sort_kernel(first, reach, count, capacity, pairs, *refs),
        in_specs=[HBM] * 6,
        out_specs=[HBM] * pieces,
        out_shape=[jax.ShapeDtypeStruct((each, width), BF16)] * pieces,
        scratch_shapes=[pltpu.VMEM((particles, lines, length), BF16)]
        + [pltpu.VMEM(a.shape, a.dtype) for a in args[1:]]
        + [
            pltpu.VMEM((length // 128, particles * lines, 128), F32),
            pltpu.VMEM((slots, width), BF16),
            pltpu.SemaphoreType.DMA((5,)),
            pltpu.SemaphoreType.DMA((2,)),
            pltpu.SemaphoreType.DMA((pieces, groups)),
        ],
        compiler_params=vmem(60),
        name="sort_particles",
    )(*args)


def joined(blocks, at):
    return jnp.concatenate([sum((ref[:, at] for ref in block[1:]), block[0][:, at]) for block in blocks], axis=0)


def score_kernel(scale, n_images, sizes, slab_lines, lines, length, *refs):
    images, refs = refs[:n_images], refs[n_images:]
    later, refs = refs[:n_images], refs[n_images:]
    early = images[0].shape[1] // length
    blocks = []
    for size in sizes:
        blocks.append(refs[:size])
        refs = refs[size:]
    out_ref, taps = refs
    info = joined(blocks, slice(lines * length, lines * length + 128))
    pairs, rows = info.shape[0], out_ref.shape[0]
    found = jnp.concatenate([ref[:, early * length :] for ref in images], axis=0).astype(F32)
    slots = found.shape[0]
    here = 4

    def stacked(line):
        refs, place = (images, line) if line < early else (later, line - early)
        return jnp.concatenate(
            [ref[:, place * length : (place + 1) * length] for ref in refs], axis=0
        )

    scores = jnp.zeros((slots, pairs), F32)
    for line in range(lines):
        block = joined(blocks, slice(line * length, (line + 1) * length))
        across = block.astype(F32).T.astype(BF16)
        scores = scores + jnp.dot(stacked(line), across, preferred_element_type=F32)

    pair_row = jnp.concatenate(
        [found[t : t + 128].T[1:2] for t in range(0, slots, 128)], axis=1
    ).astype(jnp.int32)
    onehot = lax.broadcasted_iota(jnp.int32, (pairs, slots), 0) == pair_row
    onehot = jnp.where(onehot, 1.0, 0.0).astype(BF16)
    tap = lax.dot_general(info, onehot, (((0,), (0,)), ((), ())), preferred_element_type=F32)
    put_tiles(taps, tap)
    label = tap[slab_lines * lines : slab_lines * lines + 1, :].astype(jnp.int32)
    group = lax.broadcasted_iota(jnp.int32, (rows, slots), 0) // (rows // CLASSES)
    mask = jnp.where(group == label, 1.0, 0.0).astype(BF16).reshape(rows // 16, 16, slots)

    def mixer(tap):
        tap = jnp.concatenate([tap] * (16 // slab_lines), axis=0).astype(BF16)
        return (mask * tap[None]).reshape(rows, slots)

    chosen = lax.broadcasted_iota(jnp.int32, (slots, pairs), 1) == found[:, 1:2].astype(jnp.int32)
    score = jnp.sum(jnp.where(chosen, scores, 0.0), axis=1, keepdims=True)
    weight = found[:, 3:4] / (1.0 + jnp.exp(score * (-2.0 * scale)))
    slab = jnp.zeros((rows, length), F32)
    tap_sum = jnp.zeros((slab_lines, slots), F32)
    for first in range(0, lines, here):
        mixers, contribs = [], []
        for line in range(first, first + here):
            tap = every(taps, line, slab_lines, lines)
            tap_sum = tap_sum + tap
            mixers.append(mixer(tap))
            contribs.append((weight * stacked(line).astype(F32)).astype(BF16))
        slab = slab + jnp.dot(
            jnp.concatenate(mixers, axis=1), jnp.concatenate(contribs, axis=0),
            preferred_element_type=F32,
        )
    out_ref[:, :length] = slab.astype(BF16)
    levels = lax.broadcasted_iota(jnp.int32, (slots, LEVELS), 1) == found[:, :1].astype(jnp.int32)
    levels = jnp.where(levels, weight, 0.0).astype(BF16)
    levels = jnp.dot(mixer(tap_sum), levels, preferred_element_type=F32)
    out_ref[:, length:] = levels.astype(BF16)


def score_and_spread(images, later, references, rows, slab_lines, lines, length):
    slots = sum(a.shape[0] for a in images)
    sizes = [len(a) for a in references]
    references = [a for blocks in references for a in blocks]
    return pl.pallas_call(
        lambda *refs: score_kernel(
            1.0 / math.sqrt(lines * length), len(images), sizes, slab_lines, lines, length, *refs
        ),
        out_shape=jax.ShapeDtypeStruct((rows, length + LEVELS), BF16),
        scratch_shapes=[pltpu.VMEM((slots // 128, 128, 128), F32)],
        compiler_params=vmem(24),
        name="score_and_spread",
    )(*images, *later, *references)


def level_powers(length, scale):
    level = np.arange(LEVELS)
    defocus = np.where(level < 128, 1.0 + level / 128.0, 2.0 + (level - 128) / 64.0).astype(np.float32)
    column = np.arange(length)
    folded = np.minimum(column, length - column).astype(np.float32) / np.float32(length)
    phase = (defocus * np.float32(1500.0))[:, None] * (folded * folded)[None, :] + np.float32(0.2)
    powers = np.sin(phase.astype(np.float64)) ** 2 * scale
    powers = np.where(level[:, None] <= 192, powers, 0.0)
    coarse = powers.astype(jnp.bfloat16)
    fine = (powers - coarse.astype(np.float64)).astype(jnp.bfloat16)
    return jnp.asarray(np.stack([coarse, fine]))


def pieces_of(values, count):
    pieces = []
    for _ in range(count):
        pieces.append(values.astype(BF16))
        values = values - pieces[-1].astype(F32)
    return jnp.concatenate([piece.astype(F32) for piece in pieces], axis=0).astype(BF16)


def finish_kernel(x_ref, powers_ref, slab_ref, weights_ref):
    rows, half = slab_ref.shape[0], slab_ref.shape[1] // 4
    total = jnp.sum(x_ref[...].astype(F32), axis=0)
    real, imag = total[:, :half], total[:, half : 2 * half]
    both = pieces_of(jnp.concatenate([real, imag], axis=0), 3)
    turned = jnp.dot(both, mirror(half), preferred_element_type=F32)
    turned = turned[: 2 * rows] + turned[2 * rows : 4 * rows] + turned[4 * rows :]
    first = lax.broadcasted_iota(jnp.int32, real.shape, 1) == 0
    slab_ref[:, :half] = real
    slab_ref[:, half : 2 * half] = jnp.where(first, imag[:, :1], turned[:rows])
    slab_ref[:, 2 * half : 3 * half] = jnp.where(first, 0.0, imag)
    slab_ref[:, 3 * half :] = jnp.where(first, 0.0, -turned[rows:])
    levels = pieces_of(total[:, 2 * half :], 2)
    coarse = jnp.dot(levels, powers_ref[0], preferred_element_type=F32)
    fine = jnp.dot(levels[:rows], powers_ref[1], preferred_element_type=F32)
    weights_ref[...] = coarse[:rows] + coarse[rows:] + fine


def finish(received, length, scale):
    rows = received.shape[1]
    return pl.pallas_call(
        finish_kernel,
        out_shape=(
            jax.ShapeDtypeStruct((rows, 2 * length), F32),
            jax.ShapeDtypeStruct((rows, length), F32),
        ),
        name="finish_slab",
    )(received, level_powers(length, scale))


def gather_rows(block, owners, reach, count):
    turn = lambda i: lax.ppermute(block, "owner", [(k, (k + i * count) % owners) for k in range(owners)])
    if reach != 4:
        return [(block,)] + [(turn(i),) for i in range(1, reach)]
    back, ahead = turn(1), turn(3)
    inner = range(count, 3 * count)
    up = lax.ppermute(back, "owner", [(k, k + count) for k in inner])
    down = lax.ppermute(ahead, "owner", [(k, k - count) for k in inner])
    return [(block,), (back,), (up, down), (ahead,)]


def on_device(
    images, defocus, owner_of, pair_of, shift_of, projections, interp_weights, pair_class
):
    particles, lines, length = images.shape
    owners = lax.axis_size("owner")
    capacity = 2 * particles // owners
    pairs, slab_lines, _ = interp_weights.shape
    rows = CLASSES * slab_lines
    reach = max(1, capacity // 4)
    count = owners // reach
    pieces = count if reach > 1 else 1
    early = lines // 2
    swap = lambda a, i: lax.ppermute(a, "owner", [(k, k ^ i) for k in range(owners)]) if i else a
    arrived = []
    for first, some in ((0, early), (early, lines - early)):
        moved = sort_particles(
            first, some, images, owner_of[:, 0], pair_of, shift_of, defocus, reach, count,
            reach * capacity, pairs, pieces,
        )
        if reach > 1:
            arrived.append([swap(a, i) for i, a in enumerate(moved)])
        else:
            send = lambda a: lax.all_to_all(a, "owner", split_axis=0, concat_axis=0, tiled=True)
            arrived.append([send(moved[0])])
    references = gather_rows(fold(projections, interp_weights, pair_class), owners, reach, count)
    partial = score_and_spread(*arrived, references, rows, slab_lines, lines, length)
    received = lax.all_to_all(partial, "owner", split_axis=0, concat_axis=0, tiled=True)
    return finish(
        received.reshape(owners, rows // owners, -1), length, CLASSES / (particles * owners)
    )


def solution(mesh):
    return jax.shard_map(
        on_device,
        mesh=mesh,
        in_specs=(
            P(("half", "owner"), None, None),
            P(("half", "owner")),
            P(("half", "owner"), None),
            P(("half", "owner")),
            P(("half", "owner")),
            P(("half", "owner"), None, None),
            P(("half", "owner"), None, None),
            P(("half", "owner")),
        ),
        out_specs=(P(("half", "owner"), None), P(("half", "owner"), None)),
        check_vma=False,
    )
```

```python
import math

import jax
import jax.numpy as jnp
import numpy as np
from jax import lax
from jax.experimental import pallas as pl
from jax.experimental.pallas import tpu as pltpu
from jax.sharding import PartitionSpec as P

CLASSES = 64
LEVELS = 256
F32 = jnp.float32
BF16 = jnp.bfloat16
HBM = pl.BlockSpec(memory_space=pltpu.MemorySpace.HBM)


def vmem(megabytes):
    return pltpu.CompilerParams(vmem_limit_bytes=megabytes * 1024 * 1024)


def packed_table(length):
    half = length // 2
    product = np.arange(length)[:, None] * np.arange(half + 1)[None, :] % length
    angles = product * (2.0 * math.pi / length)
    cosine, sine = np.cos(angles), -np.sin(angles)
    sine[:, 0] = cosine[:, half]
    table = np.concatenate([cosine[:, :half], sine[:, :half]], axis=1) / math.sqrt(length)
    return jnp.asarray(table, F32).astype(BF16)


def mirror(half):
    row = lax.broadcasted_iota(jnp.int32, (half, half), 0)
    column = lax.broadcasted_iota(jnp.int32, (half, half), 1)
    return jnp.where(row + column == half, 1.0, 0.0).astype(BF16)


def put_tiles(ref, values):
    for t in range(ref.shape[0]):
        ref[t] = values[:, t * 128 : (t + 1) * 128]


def every(ref, start, count, stride):
    picked = [ref[t, pl.ds(start, count, stride=stride), :] for t in range(ref.shape[0])]
    return jnp.concatenate(picked, axis=1)


def flipped(rows):
    down, across = rows.shape
    if across < 128:
        rows = jnp.concatenate([rows, jnp.zeros((down, 128 - across), F32)], axis=1)
    if down < 128:
        rows = jnp.concatenate([rows, jnp.zeros((128 - down, 128), F32)], axis=0)
    return rows.T


def short_sine(x):
    square = x * x
    total = jnp.full(x.shape, -1.0 / 39916800.0, F32)
    for factor in (1.0 / 362880.0, -1.0 / 5040.0, 1.0 / 120.0, -1.0 / 6.0, 1.0):
        total = total * square + factor
    return total * x


def sine_of(x):
    turns = jnp.floor(x * (0.5 / math.pi) + 0.5)
    x = ((x - turns * 6.28125) - turns * 0.0019340515136718750) - turns * 1.2556659145e-06
    x = jnp.where(x > 0.5 * math.pi, math.pi - x, jnp.where(x < -0.5 * math.pi, -math.pi - x, x))
    return short_sine(x)


def fold_kernel(x_ref, interp_ref, class_ref, out_ref, folded):
    pairs, width = out_ref.shape
    half = x_ref.shape[1] // 4
    lines = x_ref.shape[0] // pairs
    flip = mirror(half)
    real_low, real_high = x_ref[:, :half], x_ref[:, half : 2 * half]
    imag_low, imag_high = x_ref[:, 2 * half : 3 * half], x_ref[:, 3 * half :]
    real = real_low.astype(F32) + jnp.dot(real_high, flip, preferred_element_type=F32)
    imag = imag_low.astype(F32) - jnp.dot(imag_high, flip, preferred_element_type=F32)
    lane = lax.broadcasted_iota(jnp.int32, imag.shape, 1)
    imag = jnp.where(lane == 0, real_high.astype(F32)[:, :1], imag)
    put_tiles(folded, jnp.concatenate([real, imag], axis=1))
    for line in range(lines):
        out_ref[:, line * 2 * half : (line + 1) * 2 * half] = every(
            folded, line, pairs, lines
        ).astype(BF16)
    label = jnp.broadcast_to(class_ref[...].astype(F32), (8, pairs))
    info = flipped(jnp.concatenate([interp_ref[...].astype(F32), label], axis=0))
    out_ref[:, lines * 2 * half :] = info[:pairs].astype(BF16)


def fold(projections, interp_weights, pair_class):
    pairs, lines, width = projections.shape
    taps = interp_weights.transpose(1, 2, 0).reshape(-1, pairs)
    return pl.pallas_call(
        fold_kernel,
        out_shape=jax.ShapeDtypeStruct((pairs, lines * width // 2 + 128), BF16),
        scratch_shapes=[pltpu.VMEM((width // 256, pairs * lines, 128), F32)],
        compiler_params=vmem(12),
        name="fold_projections",
    )(projections.reshape(pairs * lines, width), taps, pair_class[None, :])


def sort_kernel(first, reach, count, capacity, pairs, *refs):
    sources, refs = refs[:6], refs[6:]
    *outs, x_ref, owner_ref, pair_ref, shift_ref, defocus_ref, table_ref, wide, sorted_ref, in_sem, x_sem, out_sem = refs
    loads = [
        pltpu.make_async_copy(a, b, in_sem.at[i])
        for i, (a, b) in enumerate(
            zip(sources[1:], (owner_ref, pair_ref, shift_ref, defocus_ref, table_ref))
        )
    ]
    parts = x_sem.shape[0]
    particles, lines, length = x_ref.shape
    share = particles // parts
    cuts = [slice(i * share, (i + 1) * share) for i in range(parts)]
    chunks = [
        pltpu.make_async_copy(sources[0].at[cut, first : first + lines], x_ref.at[cut], x_sem.at[i])
        for i, cut in enumerate(cuts)
    ]
    for copy in loads + chunks:
        copy.start()
    half = length // 2
    slots = sorted_ref.shape[0]
    each = slots // len(outs)
    row = lax.broadcasted_iota(jnp.int32, (particles, particles), 0)
    column = lax.broadcasted_iota(jnp.int32, (particles, particles), 1)
    before = jnp.where(row < column, 1.0, 0.0).astype(BF16)
    for load in loads[:4]:
        load.wait()
    me = lax.axis_index("owner")
    owner = owner_ref[...]
    bins = owner & (count - 1)
    if len(outs) > 1:
        bins = bins ^ (me & (count - 1))
    step = ((me >> (count.bit_length() - 1)) - (owner >> (count.bit_length() - 1))) & (reach - 1)
    pair = step * pairs + pair_ref[...]
    padded = -(-count // 8) * 8
    hits = lax.broadcasted_iota(jnp.int32, (padded, particles), 0) == bins
    earlier = jnp.dot(jnp.where(hits, 1.0, 0.0).astype(BF16), before, preferred_element_type=F32)
    earlier = jnp.sum(jnp.where(hits, earlier, 0.0), axis=0, keepdims=True)
    place = bins * capacity + earlier.astype(jnp.int32)
    pick = lax.broadcasted_iota(jnp.int32, (slots, particles), 0) == place
    pick = jnp.where(pick, 1.0, 0.0).astype(BF16)
    defocus = defocus_ref[...].astype(F32)
    level = jnp.where(defocus < 2.0, (defocus - 1.0) * 128.0, 128.0 + (defocus - 2.0) * 64.0)
    kind = lax.broadcasted_iota(jnp.int32, (8, particles), 0)
    facts = jnp.where(kind == 0, jnp.floor(level + 0.5), jnp.ones((8, particles), F32))
    facts = jnp.where(kind == 1, pair.astype(F32), facts)
    facts = jnp.where(kind == 2, shift_ref[...].astype(F32), facts)
    facts = flipped(jnp.where(kind == 4, defocus, facts))
    extra = 0 if first else 128
    if extra:
        picked = jnp.dot(pick, facts.astype(BF16), preferred_element_type=F32)
        sorted_ref[:, lines * length :] = picked.astype(BF16)

    column = lax.broadcasted_iota(jnp.int32, (particles, half + 128), 1)
    folded = column.astype(F32) * (1.0 / length)
    ctf = -sine_of(facts[:, 4:5] * 1500.0 * (folded * folded) + 0.2)
    shift = facts[:, 2:3].astype(jnp.int32)
    turn = (shift * column[:, :half]) & (length - 1)
    turn = jnp.where(turn >= half, turn - length, turn).astype(F32) * (2.0 * math.pi / length)
    size = jnp.abs(turn)
    mirrored = jnp.where(size > 0.5 * math.pi, math.pi - size, size)
    swing = short_sine(jnp.where(turn < 0, -mirrored, mirrored))
    cosine = ctf[:, :half] * short_sine(0.5 * math.pi - size)
    nyquist = ctf[:, half : half + 1] * (1 - 2 * (shift & 1)).astype(F32)
    cosine_imag = jnp.where(column[:, :half] == 0, nyquist, cosine)
    sine = ctf[:, :half] * swing

    loads[4].wait()
    for i, (chunk, cut) in enumerate(zip(chunks, cuts)):
        chunk.wait()
        rows = x_ref[cut].reshape(share * lines, length)
        spectra = jnp.dot(rows, table_ref[...], preferred_element_type=F32)
        spectra = spectra.astype(BF16).astype(F32)
        for t in range(length // 128):
            wide[t, i * share * lines : (i + 1) * share * lines] = spectra[:, t * 128 : (t + 1) * 128]
    groups = out_sem.shape[1]
    stores = []
    for line in range(lines):
        spectra = every(wide, line, particles, lines)
        real, imag = spectra[:, :half], spectra[:, half:]
        turned = jnp.concatenate(
            [cosine * real + sine * imag, cosine_imag * imag - sine * real], axis=1
        )
        picked = jnp.dot(pick, turned.astype(BF16), preferred_element_type=F32)
        sorted_ref[:, line * length : (line + 1) * length] = picked.astype(BF16)
        if (line + 1) % (lines // groups) == 0:
            group = line * groups // lines
            wide_group = lines // groups * length
            end = (group + 1) * wide_group + (extra if line == lines - 1 else 0)
            for j, out in enumerate(outs):
                stores.append(
                    pltpu.make_async_copy(
                        sorted_ref.at[j * each : (j + 1) * each, group * wide_group : end],
                        out.at[:, group * wide_group : end],
                        out_sem.at[j, group],
                    )
                )
                stores[-1].start()
    for store in stores:
        store.wait()


def sort_particles(first, lines, images, owner, pair, shift, defocus, reach, count, capacity, pairs, pieces):
    particles, _, length = images.shape
    slots = count * capacity
    each, width, groups = slots // pieces, lines * length + (0 if first else 128), 4
    args = [images] + [a[None, :] for a in (owner, pair, shift, defocus)]
    args.append(packed_table(length))
    return pl.pallas_call(
        lambda *refs: sort_kernel(first, reach, count, capacity, pairs, *refs),
        in_specs=[HBM] * 6,
        out_specs=[HBM] * pieces,
        out_shape=[jax.ShapeDtypeStruct((each, width), BF16)] * pieces,
        scratch_shapes=[pltpu.VMEM((particles, lines, length), BF16)]
        + [pltpu.VMEM(a.shape, a.dtype) for a in args[1:]]
        + [
            pltpu.VMEM((length // 128, particles * lines, 128), F32),
            pltpu.VMEM((slots, width), BF16),
            pltpu.SemaphoreType.DMA((5,)),
            pltpu.SemaphoreType.DMA((2,)),
            pltpu.SemaphoreType.DMA((pieces, groups)),
        ],
        compiler_params=vmem(60),
        name="sort_particles",
    )(*args)


def joined(blocks, at):
    return jnp.concatenate([sum((ref[:, at] for ref in block[1:]), block[0][:, at]) for block in blocks], axis=0)


def score_kernel(scale, n_images, sizes, slab_lines, lines, length, *refs):
    images, refs = refs[:n_images], refs[n_images:]
    later, refs = refs[:n_images], refs[n_images:]
    early = images[0].shape[1] // length
    blocks = []
    for size in sizes:
        blocks.append(refs[:size])
        refs = refs[size:]
    out_ref, taps = refs
    info = joined(blocks, slice(lines * length, lines * length + 128))
    pairs, rows = info.shape[0], out_ref.shape[0]
    found = jnp.concatenate([ref[:, early * length :] for ref in images], axis=0).astype(F32)
    slots = found.shape[0]
    here = 8

    def stacked(line):
        refs, place = (images, line) if line < early else (later, line - early)
        return jnp.concatenate(
            [ref[:, place * length : (place + 1) * length] for ref in refs], axis=0
        )

    scores = jnp.zeros((slots, pairs), F32)
    for line in range(lines):
        block = joined(blocks, slice(line * length, (line + 1) * length))
        across = block.astype(F32).T.astype(BF16)
        scores = scores + jnp.dot(stacked(line), across, preferred_element_type=F32)

    pair_row = jnp.concatenate(
        [found[t : t + 128].T[1:2] for t in range(0, slots, 128)], axis=1
    ).astype(jnp.int32)
    onehot = lax.broadcasted_iota(jnp.int32, (pairs, slots), 0) == pair_row
    onehot = jnp.where(onehot, 1.0, 0.0).astype(BF16)
    tap = lax.dot_general(info, onehot, (((0,), (0,)), ((), ())), preferred_element_type=F32)
    put_tiles(taps, tap)
    label = tap[slab_lines * lines : slab_lines * lines + 1, :].astype(jnp.int32)
    group = lax.broadcasted_iota(jnp.int32, (rows, slots), 0) // (rows // CLASSES)
    mask = jnp.where(group == label, 1.0, 0.0).astype(BF16).reshape(rows // 16, 16, slots)

    def mixer(tap):
        tap = jnp.concatenate([tap] * (16 // slab_lines), axis=0).astype(BF16)
        return (mask * tap[None]).reshape(rows, slots)

    chosen = lax.broadcasted_iota(jnp.int32, (slots, pairs), 1) == found[:, 1:2].astype(jnp.int32)
    score = jnp.sum(jnp.where(chosen, scores, 0.0), axis=1, keepdims=True)
    weight = found[:, 3:4] / (1.0 + jnp.exp(score * (-2.0 * scale)))
    slab = jnp.zeros((rows, length), F32)
    tap_sum = jnp.zeros((slab_lines, slots), F32)
    for first in range(0, lines, here):
        mixers, contribs = [], []
        for line in range(first, first + here):
            tap = every(taps, line, slab_lines, lines)
            tap_sum = tap_sum + tap
            mixers.append(mixer(tap))
            contribs.append((weight * stacked(line).astype(F32)).astype(BF16))
        slab = slab + jnp.dot(
            jnp.concatenate(mixers, axis=1), jnp.concatenate(contribs, axis=0),
            preferred_element_type=F32,
        )
    out_ref[:, :length] = slab.astype(BF16)
    levels = lax.broadcasted_iota(jnp.int32, (slots, LEVELS), 1) == found[:, :1].astype(jnp.int32)
    levels = jnp.where(levels, weight, 0.0).astype(BF16)
    levels = jnp.dot(mixer(tap_sum), levels, preferred_element_type=F32)
    out_ref[:, length:] = levels.astype(BF16)


def score_and_spread(images, later, references, rows, slab_lines, lines, length):
    slots = sum(a.shape[0] for a in images)
    sizes = [len(a) for a in references]
    references = [a for blocks in references for a in blocks]
    return pl.pallas_call(
        lambda *refs: score_kernel(
            1.0 / math.sqrt(lines * length), len(images), sizes, slab_lines, lines, length, *refs
        ),
        out_shape=jax.ShapeDtypeStruct((rows, length + LEVELS), BF16),
        scratch_shapes=[pltpu.VMEM((slots // 128, 128, 128), F32)],
        compiler_params=vmem(24),
        name="score_and_spread",
    )(*images, *later, *references)


def level_powers(length, scale):
    level = np.arange(LEVELS)
    defocus = np.where(level < 128, 1.0 + level / 128.0, 2.0 + (level - 128) / 64.0).astype(np.float32)
    column = np.arange(length)
    folded = np.minimum(column, length - column).astype(np.float32) / np.float32(length)
    phase = (defocus * np.float32(1500.0))[:, None] * (folded * folded)[None, :] + np.float32(0.2)
    powers = np.sin(phase.astype(np.float64)) ** 2 * scale
    powers = np.where(level[:, None] <= 192, powers, 0.0)
    coarse = powers.astype(jnp.bfloat16)
    fine = (powers - coarse.astype(np.float64)).astype(jnp.bfloat16)
    return jnp.asarray(np.stack([coarse, fine]))


def pieces_of(values, count):
    pieces = []
    for _ in range(count):
        pieces.append(values.astype(BF16))
        values = values - pieces[-1].astype(F32)
    return jnp.concatenate([piece.astype(F32) for piece in pieces], axis=0).astype(BF16)


def finish_kernel(x_ref, powers_ref, slab_ref, weights_ref):
    rows, half = slab_ref.shape[0], slab_ref.shape[1] // 4
    total = jnp.sum(x_ref[...].astype(F32), axis=0)
    real, imag = total[:, :half], total[:, half : 2 * half]
    both = pieces_of(jnp.concatenate([real, imag], axis=0), 3)
    turned = jnp.dot(both, mirror(half), preferred_element_type=F32)
    turned = turned[: 2 * rows] + turned[2 * rows : 4 * rows] + turned[4 * rows :]
    first = lax.broadcasted_iota(jnp.int32, real.shape, 1) == 0
    slab_ref[:, :half] = real
    slab_ref[:, half : 2 * half] = jnp.where(first, imag[:, :1], turned[:rows])
    slab_ref[:, 2 * half : 3 * half] = jnp.where(first, 0.0, imag)
    slab_ref[:, 3 * half :] = jnp.where(first, 0.0, -turned[rows:])
    levels = pieces_of(total[:, 2 * half :], 2)
    coarse = jnp.dot(levels, powers_ref[0], preferred_element_type=F32)
    fine = jnp.dot(levels[:rows], powers_ref[1], preferred_element_type=F32)
    weights_ref[...] = coarse[:rows] + coarse[rows:] + fine


def finish(received, length, scale):
    rows = received.shape[1]
    return pl.pallas_call(
        finish_kernel,
        out_shape=(
            jax.ShapeDtypeStruct((rows, 2 * length), F32),
            jax.ShapeDtypeStruct((rows, length), F32),
        ),
        name="finish_slab",
    )(received, level_powers(length, scale))


def gather_rows(block, owners, reach, count):
    turn = lambda i: lax.ppermute(block, "owner", [(k, (k + i * count) % owners) for k in range(owners)])
    if reach != 4:
        return [(block,)] + [(turn(i),) for i in range(1, reach)]
    back, ahead = turn(1), turn(3)
    inner = range(count, 3 * count)
    up = lax.ppermute(back, "owner", [(k, k + count) for k in inner])
    down = lax.ppermute(ahead, "owner", [(k, k - count) for k in inner])
    return [(block,), (back,), (up, down), (ahead,)]


def on_device(
    images, defocus, owner_of, pair_of, shift_of, projections, interp_weights, pair_class
):
    particles, lines, length = images.shape
    owners = lax.axis_size("owner")
    capacity = 2 * particles // owners
    pairs, slab_lines, _ = interp_weights.shape
    rows = CLASSES * slab_lines
    reach = max(1, capacity // 4)
    count = owners // reach
    pieces = count if reach > 1 else 1
    early = lines // 2
    swap = lambda a, i: lax.ppermute(a, "owner", [(k, k ^ i) for k in range(owners)]) if i else a
    arrived = []
    for first, some in ((0, early), (early, lines - early)):
        moved = sort_particles(
            first, some, images, owner_of[:, 0], pair_of, shift_of, defocus, reach, count,
            reach * capacity, pairs, pieces,
        )
        if reach > 1:
            arrived.append([swap(a, i) for i, a in enumerate(moved)])
        else:
            send = lambda a: lax.all_to_all(a, "owner", split_axis=0, concat_axis=0, tiled=True)
            arrived.append([send(moved[0])])
    references = gather_rows(fold(projections, interp_weights, pair_class), owners, reach, count)
    partial = score_and_spread(*arrived, references, rows, slab_lines, lines, length)
    received = lax.all_to_all(partial, "owner", split_axis=0, concat_axis=0, tiled=True)
    return finish(
        received.reshape(owners, rows // owners, -1), length, CLASSES / (particles * owners)
    )


def solution(mesh):
    return jax.shard_map(
        on_device,
        mesh=mesh,
        in_specs=(
            P(("half", "owner"), None, None),
            P(("half", "owner")),
            P(("half", "owner"), None),
            P(("half", "owner")),
            P(("half", "owner")),
            P(("half", "owner"), None, None),
            P(("half", "owner"), None, None),
            P(("half", "owner")),
        ),
        out_specs=(P(("half", "owner"), None), P(("half", "owner"), None)),
        check_vma=False,
    )
```
